512 devices in a mesh: ctx: 64 (over y, x, core), ch: 8 (over z).
Axes of the slice: x: 4, y: 8, z: 8, core: 2. Of those that a mesh axis runs over, the one named last changes fastest.
Arguments:
- grad_out: bfloat16 [8192, 4096], P('ctx', 'ch'), may hold values from -6 to 6
- inputs: bfloat16 [8192, 4096], P('ctx', 'ch'), may hold values from -0.15625 to 0.15625
- filter_taps: bfloat16 [128, 8, 4096], P('ctx', 'ch'), may hold values from -0.1875 to 0.1875
Outputs:
- grad_inputs: bfloat16 [8192, 4096], P('ctx', 'ch')
- grad_taps: float32 [128, 8, 4096], P('ctx', 'ch')
The draws below stay inside these ranges and needn't reach their ends.
All inputs are finite; a program needn't handle non-finite values.
Results may differ from the reference program's by a relative error of at most 0.0085.
Values may be sent and summed in bfloat16 or wider, within the bound.
A program may use at most 64 MiB of HBM per device.

```python
import math
import jax
import jax.numpy as jnp
from jax import lax

D = 4096
TOK_DEV = 128
FILT_DEVS = 8
FILT_LEN = 1024
SEQ_LEN = 8192
TOKENS = 8192


def steps_of(key, dims, pieces, least, top_value):
    level, own = 1.0, jax.random.fold_in(key, 6)
    for axis_at, parts in pieces:
        draws = jnp.exp(jax.random.uniform(jax.random.fold_in(own, axis_at), (parts,), jnp.float32, least / len(pieces), top_value / len(pieces)))
        level = level * jnp.repeat(draws, dims[axis_at] // parts).reshape([-1 if axis == axis_at else 1 for axis in range(len(dims))])
    return level


def bell_draw(rng, dims, scale, limit, pieces=(), kind=jnp.bfloat16):
    entries = scale * jax.random.normal(rng, dims, jnp.float32)
    if pieces:
        entries = entries * steps_of(rng, dims, pieces, -0.22, 0.18)
    return jnp.clip(entries, -limit, limit).astype(kind)


def setup_inputs(seed: int = 0) -> dict:
    key_list = jax.random.split(jax.random.key(seed), 4)
    grad_out = bell_draw(key_list[0], (TOKENS, D), 1.0, 6.0, ((0, 64), (1, 8)))
    inputs = bell_draw(key_list[1], (TOKENS, D), (1 / SEQ_LEN ** 0.5), 0.15625, ((0, 64), (1, 8)))
    filter_taps = bell_draw(key_list[2], (TOK_DEV, FILT_DEVS, D), FILT_LEN ** -0.5, 0.1875, ((0, 64), (1, 8)))
    return {"grad_out": grad_out, "inputs": inputs, "filter_taps": filter_taps}


def reference(grad_out, inputs, filter_taps):
    length = SEQ_LEN
    padded_len = 2 * length
    col_block = math.gcd(D, 256)
    col_count = D // col_block
    filter_full = jnp.transpose(filter_taps.astype(jnp.float32), (1, 0, 2)).reshape(FILT_LEN, col_count, col_block)
    filter_cols = jnp.transpose(filter_full, (1, 0, 2))
    grad_cols = jnp.transpose(grad_out.reshape(length, col_count, col_block), (1, 0, 2))
    value_cols = jnp.transpose(inputs.reshape(length, col_count, col_block), (1, 0, 2))

    def one_block(triple):
        filt_block, grad_block, value_block = triple
        filter_spec = jnp.fft.rfft(filt_block, n=padded_len, axis=0)
        grad_spec = jnp.fft.rfft(grad_block.astype(jnp.float32), n=padded_len, axis=0)
        value_spec = jnp.fft.rfft(value_block.astype(jnp.float32), n=padded_len, axis=0)
        grad_in = jnp.fft.irfft(jnp.conj(filter_spec) * grad_spec, n=padded_len, axis=0)[:length]
        tap_term = jnp.fft.irfft(grad_spec * jnp.conj(value_spec), n=padded_len, axis=0)[:FILT_LEN]
        return grad_in.astype(jnp.bfloat16), tap_term.astype(filt_block.dtype)

    grad_in, tap_total = lax.map(one_block, (filter_cols, grad_cols, value_cols))
    grad_inputs = jnp.transpose(grad_in, (1, 0, 2)).reshape(length, D)
    tap_full = jnp.transpose(tap_total, (1, 0, 2)).reshape(FILT_DEVS, TOK_DEV, D)
    grad_taps = jnp.transpose(tap_full, (1, 0, 2))
    return grad_inputs, grad_taps
```

```python
import functools
import math

import jax
import jax.numpy as jnp
from jax import lax
from jax.experimental import pallas as pl
from jax.experimental.pallas import tpu as pltpu
from jax.sharding import PartitionSpec as P

MESH = pl.DeviceIdType.MESH
F32 = jnp.float32
BF16 = jnp.bfloat16
EXACT = lax.Precision.HIGHEST


def iota(shape, axis):
    return lax.broadcasted_iota(jnp.int32, shape, axis)


def dot(a, b, ca, cb, precision=None):
    return lax.dot_general(
        a, b, (((ca,), (cb,)), ((), ())), precision=precision, preferred_element_type=F32
    )


def right(v, amount):
    amount %= v.shape[1]
    return pltpu.roll(v, amount, 1) if amount else v


def left(v, amount):
    return right(v, v.shape[1] - amount)


def kernel(
    dims, g_ref, x_ref, f_ref, out_ref, tg_ref,
    s1, r1, r2, ff, gs,
    s0, t1, ts, tr1, tx, tr2,
    dm, vs, vr1, vx, vr2, s3, o3,
    yf, o1, q1, q2,
    ysend, yrecv, xsend, xrecv, zsend, zrecv,
    tysend, tyrecv, txsend, txrecv,
    vysend, vyrecv, vxsend, vxrecv, vzsend, vzrecv,
    qysend, qyrecv, qxsend, qxrecv,
):
    ny, nu, nz, tb, cpd, rr = dims
    n = ny * nu
    width = cpd * n
    q_tiles = width // tb
    lanes = rr * cpd * nz
    tile = rr * q_tiles
    pair = 2 * cpd
    wide = (nz + 1) * tb
    half = cpd * nz

    ctx = lax.axis_index("ctx")
    z = lax.axis_index("ch")
    y = ctx // nu
    u = ctx % nu

    def y_peer(k):
        return (y + k) % ny

    def u_peer(m):
        return (u + m) % nu

    def z_peer(k):
        return (z + k) % nz

    def send(src, dst, ssem, rsem, device):
        copy = pltpu.make_async_remote_copy(
            src_ref=src, dst_ref=dst, send_sem=ssem, recv_sem=rsem,
            device_id=device, device_id_type=MESH,
        )
        copy.start()
        return copy

    def rows(ref, index, count):
        return ref.at[pl.ds(pl.multiple_of(index * count, count), count)]

    barrier = pltpu.get_barrier_semaphore()
    for k in range(1, ny):
        pl.semaphore_signal(barrier, inc=1, device_id=(y_peer(k) * nu + u, z), device_id_type=MESH)
    for m in range(1, nu):
        pl.semaphore_signal(barrier, inc=1, device_id=(y * nu + u_peer(m), z), device_id_type=MESH)
    for k in range(1, nz):
        pl.semaphore_signal(barrier, inc=1, device_id=(ctx, z_peer(k)), device_id_type=MESH)

    taps_in = f_ref[...].astype(F32)
    for to in range(nz):
        for r in range(rr):
            for q in range(q_tiles):
                at = to * width + q * tb
                s0[to * tile + r * q_tiles + q : to * tile + r * q_tiles + q + 1, :] = taps_in[r : r + 1, at : at + tb]

    g_t = g_ref[...].astype(F32).T.reshape(n, cpd, tb)
    x_t = x_ref[...].astype(F32).T.reshape(n, cpd, tb)
    s1[...] = jnp.concatenate([g_t, x_t], axis=1).astype(BF16)
    ff[n * pair :, :] = jnp.zeros((nz * pair, tb), F32)

    pl.semaphore_wait(barrier, ny + nu + nz - 3)

    pending = []
    zc = []
    for k in range(1, nz):
        zc.append(send(rows(s0, z_peer(k), tile), rows(t1, z, tile), zsend.at[k], zrecv.at[k], (ctx, z_peer(k))))
    yc = {}
    for k in sorted(range(1, ny), key=lambda k: -min(k, ny - k)):
        yc[k] = send(rows(s1, y_peer(k), nu), rows(r1, y, nu), ysend.at[k], yrecv.at[k], (y_peer(k) * nu + u, z))
    for m in range(1, nu):
        send(s1.at[y * nu + u_peer(m)], r2.at[y * nu + u], xsend.at[m], xrecv.at[m], (y * nu + u_peer(m), z))
    r2[pl.ds(y * nu + u, 1)] = s1[pl.ds(y * nu + u, 1)]

    def forward(k):
        yc[k].wait_recv()
        src = (y + ny - k) % ny
        for m in range(1, nu):
            send(r1.at[src * nu + u_peer(m)], r2.at[src * nu + u], xsend.at[m], xrecv.at[m], (y * nu + u_peer(m), z))
        r2[pl.ds(src * nu + u, 1)] = r1[pl.ds(src * nu + u, 1)]

    order = sorted(range(1, ny), key=lambda k: min(k, ny - k))

    t1[pl.ds(pl.multiple_of(z * tile, tile), tile), :] = s0[pl.ds(pl.multiple_of(z * tile, tile), tile), :]
    for copy in zc:
        copy.wait_recv()
    taps = jnp.concatenate([t1[pl.ds(q, nz * rr, stride=q_tiles), :] for q in range(q_tiles)], axis=1)
    lane_r = iota((lanes, nz * rr), 0) // half
    lane_s = iota((lanes, nz * rr), 0) % nz
    spread = (iota((lanes, nz * rr), 1) == lane_s * rr + lane_r).astype(BF16)
    own_channel = (iota((lanes, width), 0) // nz) % cpd == iota((lanes, width), 1) % cpd
    group = (iota((n, width), 0) == iota((n, width), 1) // cpd).astype(BF16)
    spread_taps = jnp.where(own_channel, dot(spread, taps.astype(BF16), 1, 0), 0.0)
    ts[...] = dot(group, spread_taps.astype(BF16), 1, 1)
    tyc = []
    for k in range(1, ny):
        tyc.append(send(rows(ts, y_peer(k), nu), rows(tr1, y, nu), tysend.at[k], tyrecv.at[k], (y_peer(k) * nu + u, z)))
    tr1[pl.ds(pl.multiple_of(y * nu, nu), nu), :] = ts[pl.ds(pl.multiple_of(y * nu, nu), nu), :]

    for k in order:
        forward(k)

    for copy in tyc:
        copy.wait_recv()
    for to in range(nu):
        tx[to * ny : (to + 1) * ny, :] = tr1[pl.ds(to, ny, stride=nu), :]
    txc = []
    for m in range(1, nu):
        txc.append(send(rows(tx, u_peer(m), ny), rows(tr2, u, ny), txsend.at[m], txrecv.at[m], (y * nu + u_peer(m), z)))
    tr2[pl.ds(pl.multiple_of(u * ny, ny), ny), :] = tx[pl.ds(pl.multiple_of(u * ny, ny), ny), :]

    for m in range(1, nu):
        pltpu.make_async_copy(r2.at[pl.ds(0, ny)], r2.at[pl.ds(0, ny)], xrecv.at[m]).wait()
    ff[: n * pair, :] = r2[...].astype(F32).reshape(n * pair, tb)

    sub = iota((8, wide), 0)
    for c in range(cpd):
        shifted = jnp.concatenate(
            [ff[pl.ds(c + pair * d, n, stride=pair), :].astype(BF16) for d in range(nz + 1)], axis=1
        )
        gs[c] = shifted
        values = ff[pl.ds(cpd + c, n, stride=pair), :].T.astype(BF16)
        pairs = dot(values, shifted, 1, 0)
        parts = [pairs[8 * a : 8 * a + 8] for a in range(tb // 8)]
        shift = 8
        while len(parts) > 1:
            parts = [parts[i] + left(parts[i + 1], shift) for i in range(0, len(parts), 2)]
            shift *= 2
        total = parts[0]
        for bit in (1, 2, 4):
            total = jnp.where((sub & bit) != 0, left(total, bit), total)
        total = jnp.sum(total, axis=0, keepdims=True)
        for s in range(nz):
            dm[c * nz + s : c * nz + s + 1, :] = total[:, s * tb : (s + 1) * tb]

    spots = jnp.concatenate([dm[...]] * rr, axis=0)
    spots = jnp.where(iota((lanes, tb), 1) % rr == iota((lanes, tb), 0) // half, spots, 0.0)
    owner = (iota((n, tb), 1) // rr == iota((n, tb), 0)).astype(F32)
    vs[...] = dot(owner, spots, 1, 1, EXACT)
    vyc = []
    for k in range(1, ny):
        vyc.append(send(rows(vs, y_peer(k), nu), rows(vr1, y, nu), vysend.at[k], vyrecv.at[k], (y_peer(k) * nu + u, z)))
    vr1[pl.ds(pl.multiple_of(y * nu, nu), nu), :] = vs[pl.ds(pl.multiple_of(y * nu, nu), nu), :]

    for copy in txc:
        copy.wait_recv()
    from_block = (iota((n, tb), 0) % ny) * nu + iota((n, tb), 0) // ny
    place = (iota((n, tb), 1) // rr == from_block).astype(BF16)
    placed = dot(tr2[...].T.astype(BF16), place, 1, 0)
    placed = jnp.where(iota((lanes, tb), 1) % rr == iota((lanes, tb), 0) // half, placed, 0.0)
    own_taps = placed[:half]
    for r in range(1, rr):
        own_taps = own_taps + placed[r * half : (r + 1) * half]

    for c in range(cpd):
        row = jnp.concatenate(
            [own_taps[c * nz + s : c * nz + s + 1] for s in range(nz)] + [jnp.zeros((1, tb), F32)], axis=1
        )
        base = jnp.broadcast_to(row, (8, wide))
        for bit in (1, 2, 4):
            base = jnp.where((sub & bit) != 0, right(base, bit), base)
        toeplitz = jnp.concatenate([right(base, 8 * a) for a in range(tb // 8)], axis=0).astype(BF16)
        yf[pl.ds(c, n, stride=cpd), :] = dot(gs[c], toeplitz, 1, 1)
    o1[...] = yf[...].astype(BF16).reshape(n, cpd, tb)

    qyc = {}
    for k in sorted(range(1, ny), key=lambda k: -min(k, ny - k)):
        qyc[k] = send(rows(o1, y_peer(k), nu), rows(q1, y, nu), qysend.at[k], qyrecv.at[k], (y_peer(k) * nu + u, z))
    for m in range(1, nu):
        send(o1.at[y * nu + u_peer(m)], q2.at[y * nu + u], qxsend.at[m], qxrecv.at[m], (y * nu + u_peer(m), z))
    q2[pl.ds(y * nu + u, 1)] = o1[pl.ds(y * nu + u, 1)]

    for copy in vyc:
        copy.wait_recv()
    for to in range(nu):
        vx[to * ny : (to + 1) * ny, :] = vr1[pl.ds(to, ny, stride=nu), :]
    vxc = []
    for m in range(1, nu):
        vxc.append(send(rows(vx, u_peer(m), ny), rows(vr2, u, ny), vxsend.at[m], vxrecv.at[m], (y * nu + u_peer(m), z)))
    vr2[pl.ds(pl.multiple_of(u * ny, ny), ny), :] = vx[pl.ds(pl.multiple_of(u * ny, ny), ny), :]

    for k in order:
        qyc[k].wait_recv()
        src = (y + ny - k) % ny
        for m in range(1, nu):
            send(q1.at[src * nu + u_peer(m)], q2.at[src * nu + u], qxsend.at[m], qxrecv.at[m], (y * nu + u_peer(m), z))
        q2[pl.ds(src * nu + u, 1)] = q1[pl.ds(src * nu + u, 1)]

    for copy in vxc:
        copy.wait_recv()
    regroup = (iota((n, width), 1) // cpd == (iota((n, width), 0) % ny) * nu + iota((n, width), 0) // ny).astype(F32)
    picked = jnp.where(own_channel, dot(vr2[...].T, regroup, 1, 0, EXACT), 0.0)
    pick_r = iota((nz * rr, lanes), 1) // half
    pick_s = iota((nz * rr, lanes), 1) % nz
    collect = (iota((nz * rr, lanes), 0) == pick_s * rr + pick_r).astype(F32)
    tap_rows = dot(collect, picked, 1, 0, EXACT)
    for q in range(q_tiles):
        s3[pl.ds(q, nz * rr, stride=q_tiles), :] = tap_rows[:, q * tb : (q + 1) * tb]
    vzc = []
    for k in range(1, nz):
        vzc.append(send(rows(s3, z_peer(k), tile), rows(o3, z, tile), vzsend.at[k], vzrecv.at[k], (ctx, z_peer(k))))
    o3[pl.ds(pl.multiple_of(z * tile, tile), tile), :] = s3[pl.ds(pl.multiple_of(z * tile, tile), tile), :]

    for m in range(1, nu):
        pltpu.make_async_copy(q2.at[pl.ds(0, ny)], q2.at[pl.ds(0, ny)], qxrecv.at[m]).wait()
    out_ref[...] = q2[...].astype(F32).reshape(width, tb).T.astype(BF16)

    for copy in vzc:
        copy.wait_recv()
    for src in range(nz):
        for r in range(rr):
            for q in range(q_tiles):
                at = src * width + q * tb
                row = src * tile + r * q_tiles + q
                tg_ref[r : r + 1, at : at + tb] = o3[row : row + 1, :]

    for copy in zc + list(yc.values()) + tyc + txc + vyc + list(qyc.values()) + vxc + vzc:
        copy.wait_send()
    for m in range(1, nu):
        pltpu.make_async_copy(r2.at[pl.ds(0, ny)], r2.at[pl.ds(0, ny)], xsend.at[m]).wait()
        pltpu.make_async_copy(q2.at[pl.ds(0, ny)], q2.at[pl.ds(0, ny)], qxsend.at[m]).wait()


def shards(grad_out, inputs, filter_taps):
    tb, width = grad_out.shape
    n = lax.axis_size("ctx")
    nz = lax.axis_size("ch")
    nu = math.isqrt(n)
    ny = n // nu
    rr = filter_taps.shape[0]
    cpd = width // n
    tile = rr * width // tb
    lanes = rr * cpd * nz
    vmem = pltpu.VMEM
    dma = pltpu.SemaphoreType.DMA
    whole = pl.BlockSpec(memory_space=vmem)
    grad_inputs, grad_taps = pl.pallas_call(
        functools.partial(kernel, (ny, nu, nz, tb, cpd, rr)),
        out_shape=(
            jax.ShapeDtypeStruct((tb, width), BF16),
            jax.ShapeDtypeStruct((rr, nz * width), F32),
        ),
        in_specs=[whole] * 3,
        out_specs=(whole, whole),
        scratch_shapes=[
            vmem((n, 2 * cpd, tb), BF16),
            vmem((n, 2 * cpd, tb), BF16),
            vmem((n, 2 * cpd, tb), BF16),
            vmem(((n + nz) * 2 * cpd, tb), F32),
            vmem((cpd, n, (nz + 1) * tb), BF16),
            vmem((nz * tile, tb), F32),
            vmem((nz * tile, tb), F32),
            vmem((n, lanes), F32),
            vmem((n, lanes), F32),
            vmem((n, lanes), F32),
            vmem((n, lanes), F32),
            vmem((cpd * nz, tb), F32),
            vmem((n, lanes), F32),
            vmem((n, lanes), F32),
            vmem((n, lanes), F32),
            vmem((n, lanes), F32),
            vmem((nz * tile, tb), F32),
            vmem((nz * tile, tb), F32),
            vmem((n * cpd, tb), F32),
            vmem((n, cpd, tb), BF16),
            vmem((n, cpd, tb), BF16),
            vmem((n, cpd, tb), BF16),
            dma((ny,)), dma((ny,)), dma((nu,)), dma((nu,)), dma((nz,)), dma((nz,)),
            dma((ny,)), dma((ny,)), dma((nu,)), dma((nu,)),
            dma((ny,)), dma((ny,)), dma((nu,)), dma((nu,)), dma((nz,)), dma((nz,)),
            dma((ny,)), dma((ny,)), dma((nu,)), dma((nu,)),
        ],
        compiler_params=pltpu.CompilerParams(collective_id=0, has_side_effects=True),
    )(grad_out, inputs, filter_taps.reshape(rr, nz * width))
    return grad_inputs, grad_taps.reshape(rr, 1, nz * width)


def solution(mesh):
    placed = (P("ctx", "ch"), P("ctx", "ch"), P("ctx", "ch", None))
    return jax.shard_map(
        shards,
        mesh=mesh,
        in_specs=placed,
        out_specs=(P("ctx", "ch"), P("ctx", "ch", None)),
        check_vma=False,
    )
```

```python
import functools
import math

import jax
import jax.numpy as jnp
from jax import lax
from jax.experimental import pallas as pl
from jax.experimental.pallas import tpu as pltpu
from jax.sharding import PartitionSpec as P

MESH = pl.DeviceIdType.MESH
F32 = jnp.float32
BF16 = jnp.bfloat16
EXACT = lax.Precision.HIGHEST


def iota(shape, axis):
    return lax.broadcasted_iota(jnp.int32, shape, axis)


def dot(a, b, ca, cb, precision=None):
    return lax.dot_general(
        a, b, (((ca,), (cb,)), ((), ())), precision=precision, preferred_element_type=F32
    )


def right(v, amount):
    amount %= v.shape[1]
    return pltpu.roll(v, amount, 1) if amount else v


def left(v, amount):
    return right(v, v.shape[1] - amount)


def kernel(
    dims, g_hbm, x_hbm, f_hbm, out_ref, tg_ref,
    gv, xv, fv, s1, r2, ff, gs,
    s0, t1, ts, tr,
    dm, vs, vr, s3, o3,
    yf, o1, q2,
    insem, xsend, xrecv, zsend, zrecv, tsend, trecv, vsend, vrecv, vzsend, vzrecv, qsend, qrecv,
):
    n, ny, nx, nc, nz, tb, cpd, rr = dims
    nu = nx * nc
    width = cpd * n
    q_tiles = width // tb
    lanes = rr * cpd * nz
    tile = rr * q_tiles
    pair = 2 * cpd
    wide = (nz + 1) * tb
    half = cpd * nz

    ctx = lax.axis_index("ctx")
    z = lax.axis_index("ch")
    y = ctx // nu
    x = (ctx // nc) % nx
    core = ctx % nc

    def hops(offset):
        dy, dx, _ = offset
        return min(dy, ny - dy) + min(dx, nx - dx)

    offsets = [(dy, dx, dc) for dc in range(nc) for dx in range(nx) for dy in range(ny)][1:]
    offsets.sort(key=lambda o: -hops(o))
    y_at = [((y + d) % ny) * nu for d in range(ny)]
    u_at = {(dx, dc): ((x + dx) % nx) * nc + (core + dc) % nc for dx in range(nx) for dc in range(nc)}
    peers = [y_at[dy] + u_at[dx, dc] for dy, dx, dc in offsets]
    z_peers = [(z + k) % nz for k in range(nz)]

    barrier = pltpu.get_barrier_semaphore()
    for peer in peers:
        pl.semaphore_signal(barrier, inc=1, device_id=(peer, z), device_id_type=MESH)
    for k in range(1, nz):
        pl.semaphore_signal(barrier, inc=1, device_id=(ctx, z_peers[k]), device_id_type=MESH)

    loads = [
        pltpu.make_async_copy(f_hbm, fv, insem.at[2]),
        pltpu.make_async_copy(g_hbm, gv, insem.at[0]),
        pltpu.make_async_copy(x_hbm, xv, insem.at[1]),
    ]
    for load in loads:
        load.start()

    def send(src, dst, ssem, rsem, device):
        copy = pltpu.make_async_remote_copy(
            src_ref=src, dst_ref=dst, send_sem=ssem, recv_sem=rsem,
            device_id=device, device_id_type=MESH,
        )
        copy.start()
        return copy

    def rows(ref, index, count):
        return ref.at[pl.ds(pl.multiple_of(index * count, count), count)]

    def wait_all(ref, sem):
        pltpu.make_async_copy(ref.at[pl.ds(0, n - 1)], ref.at[pl.ds(0, n - 1)], sem).wait()

    loads[0].wait()
    taps_in = fv[...].astype(F32)
    for to in range(nz):
        for r in range(rr):
            for q in range(q_tiles):
                at = to * width + q * tb
                s0[to * tile + r * q_tiles + q : to * tile + r * q_tiles + q + 1, :] = taps_in[r : r + 1, at : at + tb]

    loads[1].wait()
    loads[2].wait()
    g_t = gv[...].astype(F32).T.reshape(n, cpd, tb)
    x_t = xv[...].astype(F32).T.reshape(n, cpd, tb)
    s1[...] = jnp.concatenate([g_t, x_t], axis=1).astype(BF16)
    ff[n * pair :, :] = jnp.zeros((nz * pair, tb), F32)

    pl.semaphore_wait(barrier, n - 1 + nz - 1)

    zc = []
    for k in range(1, nz):
        zc.append(send(rows(s0, z_peers[k], tile), rows(t1, z, tile), zsend.at[k], zrecv.at[k], (ctx, z_peers[k])))
    for peer in peers:
        send(s1.at[peer], r2.at[ctx], xsend, xrecv, (peer, z))
    r2[pl.ds(ctx, 1)] = s1[pl.ds(ctx, 1)]
    t1[pl.ds(pl.multiple_of(z * tile, tile), tile), :] = s0[pl.ds(pl.multiple_of(z * tile, tile), tile), :]

    for copy in zc:
        copy.wait_recv()
    taps = jnp.concatenate([t1[pl.ds(q, nz * rr, stride=q_tiles), :] for q in range(q_tiles)], axis=1)
    lane_r = iota((lanes, nz * rr), 0) // half
    lane_s = iota((lanes, nz * rr), 0) % nz
    spread = (iota((lanes, nz * rr), 1) == lane_s * rr + lane_r).astype(BF16)
    own_channel = (iota((lanes, width), 0) // nz) % cpd == iota((lanes, width), 1) % cpd
    group = iota((n, width), 0) == iota((n, width), 1) // cpd
    spread_taps = jnp.where(own_channel, dot(spread, taps.astype(BF16), 1, 0), 0.0)
    ts[:, 0, :] = dot(group.astype(BF16), spread_taps.astype(BF16), 1, 1)
    for peer in peers:
        send(ts.at[peer], tr.at[ctx], tsend, trecv, (peer, z))
    tr[pl.ds(ctx, 1)] = ts[pl.ds(ctx, 1)]

    wait_all(r2, xrecv)
    ff[: n * pair, :] = r2[...].astype(F32).reshape(n * pair, tb)

    sub = iota((8, wide), 0)
    for c in range(cpd):
        shifted = jnp.concatenate(
            [ff[pl.ds(c + pair * d, n, stride=pair), :].astype(BF16) for d in range(nz + 1)], axis=1
        )
        gs[c] = shifted
        values = ff[pl.ds(cpd + c, n, stride=pair), :].T.astype(BF16)
        pairs = dot(values, shifted, 1, 0)
        parts = [pairs[8 * a : 8 * a + 8] for a in range(tb // 8)]
        shift = 8
        while len(parts) > 1:
            parts = [parts[i] + left(parts[i + 1], shift) for i in range(0, len(parts), 2)]
            shift *= 2
        total = parts[0]
        for bit in (1, 2, 4):
            total = jnp.where((sub & bit) != 0, left(total, bit), total)
        total = jnp.sum(total, axis=0, keepdims=True)
        for s in range(nz):
            dm[c * nz + s : c * nz + s + 1, :] = total[:, s * tb : (s + 1) * tb]

    spots = jnp.concatenate([dm[...]] * rr, axis=0)
    spots = jnp.where(iota((lanes, tb), 1) % rr == iota((lanes, tb), 0) // half, spots, 0.0)
    owner = (iota((n, tb), 1) // rr == iota((n, tb), 0)).astype(F32)
    vs[:, 0, :] = dot(owner, spots, 1, 1, EXACT)
    for peer in peers:
        send(vs.at[peer], vr.at[ctx], vsend, vrecv, (peer, z))
    vr[pl.ds(ctx, 1)] = vs[pl.ds(ctx, 1)]

    wait_all(tr, trecv)
    placed = dot(tr[:, 0, :].T.astype(BF16), owner.astype(BF16), 1, 0)
    placed = jnp.where(iota((lanes, tb), 1) % rr == iota((lanes, tb), 0) // half, placed, 0.0)
    own_taps = placed[:half]
    for r in range(1, rr):
        own_taps = own_taps + placed[r * half : (r + 1) * half]

    for c in range(cpd):
        row = jnp.concatenate(
            [own_taps[c * nz + s : c * nz + s + 1] for s in range(nz)] + [jnp.zeros((1, tb), F32)], axis=1
        )
        base = jnp.broadcast_to(row, (8, wide))
        for bit in (1, 2, 4):
            base = jnp.where((sub & bit) != 0, right(base, bit), base)
        toeplitz = jnp.concatenate([right(base, 8 * a) for a in range(tb // 8)], axis=0).astype(BF16)
        yf[pl.ds(c, n, stride=cpd), :] = dot(gs[c], toeplitz, 1, 1)
    o1[...] = yf[...].astype(BF16).reshape(n, cpd, tb)

    for peer in peers:
        send(o1.at[peer], q2.at[ctx], qsend, qrecv, (peer, z))
    q2[pl.ds(ctx, 1)] = o1[pl.ds(ctx, 1)]

    wait_all(vr, vrecv)
    picked = jnp.where(own_channel, dot(vr[:, 0, :].T, group.astype(F32), 1, 0, EXACT), 0.0)
    pick_r = iota((nz * rr, lanes), 1) // half
    pick_s = iota((nz * rr, lanes), 1) % nz
    collect = (iota((nz * rr, lanes), 0) == pick_s * rr + pick_r).astype(F32)
    tap_rows = dot(collect, picked, 1, 0, EXACT)
    for q in range(q_tiles):
        s3[pl.ds(q, nz * rr, stride=q_tiles), :] = tap_rows[:, q * tb : (q + 1) * tb]
    vzc = []
    for k in range(1, nz):
        vzc.append(send(rows(s3, z_peers[k], tile), rows(o3, z, tile), vzsend.at[k], vzrecv.at[k], (ctx, z_peers[k])))
    o3[pl.ds(pl.multiple_of(z * tile, tile), tile), :] = s3[pl.ds(pl.multiple_of(z * tile, tile), tile), :]

    wait_all(q2, qrecv)
    out_ref[...] = q2[...].astype(F32).reshape(width, tb).T.astype(BF16)

    for copy in vzc:
        copy.wait_recv()
    for src in range(nz):
        for r in range(rr):
            for q in range(q_tiles):
                at = src * width + q * tb
                row = src * tile + r * q_tiles + q
                tg_ref[r, :, at : at + tb] = o3[row : row + 1, :]

    for copy in zc + vzc:
        copy.wait_send()
    for ref, sem in ((s1, xsend), (ts, tsend), (vs, vsend), (o1, qsend)):
        wait_all(ref, sem)


def shards(grad_out, inputs, filter_taps):
    tb, width = grad_out.shape
    n = lax.axis_size("ctx")
    nz = lax.axis_size("ch")
    nu = math.isqrt(n)
    ny = n // nu
    nc = 2
    nx = nu // nc
    rr = filter_taps.shape[0]
    cpd = width // n
    tile = rr * width // tb
    lanes = rr * cpd * nz
    vmem = pltpu.VMEM
    dma = pltpu.SemaphoreType.DMA
    return pl.pallas_call(
        functools.partial(kernel, (n, ny, nx, nc, nz, tb, cpd, rr)),
        out_shape=(
            pltpu.VMEM((tb, width), BF16),
            pltpu.VMEM((rr, 1, nz * width), F32),
        ),
        in_specs=[pl.BlockSpec(memory_space=pl.ANY)] * 3,
        out_specs=[pl.BlockSpec(memory_space=vmem)] * 2,
        scratch_shapes=[
            vmem((tb, width), BF16),
            vmem((tb, width), BF16),
            vmem((rr, nz * width), BF16),
            vmem((n, 2 * cpd, tb), BF16),
            vmem((n, 2 * cpd, tb), BF16),
            vmem(((n + nz) * 2 * cpd, tb), F32),
            vmem((cpd, n, (nz + 1) * tb), BF16),
            vmem((nz * tile, tb), F32),
            vmem((nz * tile, tb), F32),
            vmem((n, 1, lanes), F32),
            vmem((n, 1, lanes), F32),
            vmem((cpd * nz, tb), F32),
            vmem((n, 1, lanes), F32),
            vmem((n, 1, lanes), F32),
            vmem((nz * tile, tb), F32),
            vmem((nz * tile, tb), F32),
            vmem((n * cpd, tb), F32),
            vmem((n, cpd, tb), BF16),
            vmem((n, cpd, tb), BF16),
            dma((3,)), dma, dma, dma((nz,)), dma((nz,)), dma, dma, dma, dma, dma((nz,)), dma((nz,)), dma, dma,
        ],
        compiler_params=pltpu.CompilerParams(collective_id=0, has_side_effects=True),
    )(grad_out, inputs, filter_taps.reshape(rr, nz * width))


def solution(mesh):
    placed = (P("ctx", "ch"), P("ctx", "ch"), P("ctx", "ch", None))
    return jax.shard_map(
        shards,
        mesh=mesh,
        in_specs=placed,
        out_specs=(P("ctx", "ch"), P("ctx", "ch", None)),
        check_vma=False,
    )
```

```python
import functools
import math

import jax
import jax.numpy as jnp
import numpy as np
from jax import lax
from jax.experimental import pallas as pl
from jax.experimental.pallas import tpu as pltpu
from jax.sharding import PartitionSpec as P

MESH = pl.DeviceIdType.MESH
F32 = jnp.float32
BF16 = jnp.bfloat16
EXACT = lax.Precision.HIGHEST


def iota(shape, axis):
    return lax.broadcasted_iota(jnp.int32, shape, axis)


def dot(a, b, ca, cb, precision=None):
    return lax.dot_general(
        a, b, (((ca,), (cb,)), ((), ())), precision=precision, preferred_element_type=F32
    )


def halves(v):
    upper = v.astype(BF16)
    return upper, (v - upper.astype(F32)).astype(BF16)


def dft_tables(tb):
    place = np.arange(tb)[:, None]
    freq = np.arange(tb)[None, :]
    angle = (place * freq % (2 * tb)) * (np.pi / tb)
    parity = np.where(place % 2 == 0, 1.0, -1.0)
    forward = np.concatenate([np.cos(angle), np.where(freq == 0, parity, -np.sin(angle))], axis=1)
    weight = np.where(np.arange(2 * tb) % tb == 0, 0.5, 1.0) / tb
    backward = (forward * weight).T

    def split(table):
        table = table.astype(np.float32)
        upper = table.astype(BF16)
        return upper, (table - upper.astype(np.float32)).astype(BF16)

    fu, fl = split(forward)
    bu, bl = split(backward)
    return np.concatenate([fu, fl], axis=0), np.concatenate([bu, bu, bl], axis=0)


def kernel(
    dims, g_hbm, x_hbm, f_hbm, fwd_hbm, inv_hbm, out_ref, tg_ref,
    gv, xv, fv, fwd, inv, s1, r2, sp,
    s0, t1, ts, tr,
    pacc, kt, vs, vr, s3, o3,
    ys, o1, q2,
    insem, xsend, xrecv, zsend, zrecv, tsend, trecv, vsend, vrecv, vzsend, vzrecv, qsend, qrecv,
):
    n, ny, nx, nc, nz, tb, cpd, rr = dims
    nu = nx * nc
    width = cpd * n
    q_tiles = width // tb
    lanes = rr * cpd * nz
    tile = rr * q_tiles
    pair = 2 * cpd
    half = cpd * nz

    ctx = lax.axis_index("ctx")
    z = lax.axis_index("ch")
    y = ctx // nu
    x = (ctx // nc) % nx
    core = ctx % nc

    def hops(offset):
        dy, dx, _ = offset
        return min(dy, ny - dy) + min(dx, nx - dx)

    offsets = [(dy, dx, dc) for dc in range(nc) for dx in range(nx) for dy in range(ny)][1:]
    offsets.sort(key=lambda o: -hops(o))
    y_at = [((y + d) % ny) * nu for d in range(ny)]
    u_at = {(dx, dc): ((x + dx) % nx) * nc + (core + dc) % nc for dx in range(nx) for dc in range(nc)}
    peers = [y_at[dy] + u_at[dx, dc] for dy, dx, dc in offsets]
    z_peers = [(z + k) % nz for k in range(nz)]

    barrier = pltpu.get_barrier_semaphore()
    for peer in peers:
        pl.semaphore_signal(barrier, inc=1, device_id=(peer, z), device_id_type=MESH)
    for k in range(1, nz):
        pl.semaphore_signal(barrier, inc=1, device_id=(ctx, z_peers[k]), device_id_type=MESH)

    loads = [
        pltpu.make_async_copy(f_hbm, fv, insem.at[2]),
        pltpu.make_async_copy(g_hbm, gv, insem.at[0]),
        pltpu.make_async_copy(x_hbm, xv, insem.at[1]),
        pltpu.make_async_copy(fwd_hbm, fwd, insem.at[3]),
        pltpu.make_async_copy(inv_hbm, inv, insem.at[4]),
    ]
    for load in loads:
        load.start()

    def send(src, dst, ssem, rsem, device):
        copy = pltpu.make_async_remote_copy(
            src_ref=src, dst_ref=dst, send_sem=ssem, recv_sem=rsem,
            device_id=device, device_id_type=MESH,
        )
        copy.start()
        return copy

    def rows(ref, index, count):
        return ref.at[pl.ds(pl.multiple_of(index * count, count), count)]

    def wait_all(ref, sem):
        pltpu.make_async_copy(ref.at[pl.ds(0, n - 1)], ref.at[pl.ds(0, n - 1)], sem).wait()

    loads[0].wait()
    taps_in = fv[...].astype(F32)
    for to in range(nz):
        for r in range(rr):
            for q in range(q_tiles):
                at = to * width + q * tb
                s0[to * tile + r * q_tiles + q : to * tile + r * q_tiles + q + 1, :] = taps_in[r : r + 1, at : at + tb]

    loads[1].wait()
    loads[2].wait()
    g_t = gv[...].astype(F32).T.reshape(n, cpd, tb)
    x_t = xv[...].astype(F32).T.reshape(n, cpd, tb)
    s1[...] = jnp.concatenate([g_t, x_t], axis=1).astype(BF16)
    sp[n * pair :, :] = jnp.zeros((nz * pair, 2 * tb), F32)

    pl.semaphore_wait(barrier, n - 1 + nz - 1)

    zc = []
    for k in range(1, nz):
        zc.append(send(rows(s0, z_peers[k], tile), rows(t1, z, tile), zsend.at[k], zrecv.at[k], (ctx, z_peers[k])))
    for peer in peers:
        send(s1.at[peer], r2.at[ctx], xsend, xrecv, (peer, z))
    r2[pl.ds(ctx, 1)] = s1[pl.ds(ctx, 1)]
    t1[pl.ds(pl.multiple_of(z * tile, tile), tile), :] = s0[pl.ds(pl.multiple_of(z * tile, tile), tile), :]

    for copy in zc:
        copy.wait_recv()
    taps = jnp.concatenate([t1[pl.ds(q, nz * rr, stride=q_tiles), :] for q in range(q_tiles)], axis=1)
    lane_r = iota((lanes, nz * rr), 0) // half
    lane_s = iota((lanes, nz * rr), 0) % half // cpd
    spread = (iota((lanes, nz * rr), 1) == lane_s * rr + lane_r).astype(BF16)
    own_channel = iota((lanes, width), 0) % cpd == iota((lanes, width), 1) % cpd
    group = iota((n, width), 0) == iota((n, width), 1) // cpd
    spread_taps = jnp.where(own_channel, dot(spread, taps.astype(BF16), 1, 0), 0.0)
    ts[:, 0, :] = dot(group.astype(BF16), spread_taps.astype(BF16), 1, 1)
    for peer in peers:
        send(ts.at[peer], tr.at[ctx], tsend, trecv, (peer, z))
    tr[pl.ds(ctx, 1)] = ts[pl.ds(ctx, 1)]

    wait_all(r2, xrecv)
    def to_spectrum(v):
        return dot(jnp.concatenate([v, v], axis=1), fwd[...], 1, 0)

    def from_spectrum(v):
        upper, lower = halves(v)
        return dot(jnp.concatenate([upper, lower, upper], axis=1), inv[...], 1, 0)

    loads[3].wait()
    loads[4].wait()
    sp[: n * pair, :] = to_spectrum(r2[...].reshape(n * pair, tb))
    lane = iota((cpd, tb), 1)
    parity = jnp.where(lane % 2 == 0, 1.0, -1.0)
    edge = lane == 0

    def spec_at(block, first):
        at = pl.ds(pl.multiple_of(block * pair + first, cpd), cpd)
        return sp[at, :tb], sp[at, tb:]

    group_d = 3

    for d0 in range(0, nz + 1, group_d):
        ds = range(d0, min(d0 + group_d, nz + 1))

        def step(i, sums, ds=ds):
            sums = list(sums)
            xs = [spec_at(i * 4 + j, cpd) for j in range(4)]
            for at in range(ds[0], ds[-1] + 4):
                gr, gi = spec_at(i * 4 + at, 0)
                for e, d in enumerate(ds):
                    if 0 <= at - d < 4:
                        xr, xi = xs[at - d]
                        sums[4 * e] += xr * gr
                        sums[4 * e + 1] += xi * gi
                        sums[4 * e + 2] += xr * gi
                        sums[4 * e + 3] += xi * gr
            return tuple(sums)

        zero = jnp.zeros((cpd, tb), F32)
        sums = lax.fori_loop(0, n // 4, step, (zero,) * (4 * len(ds)))
        for e, d in enumerate(ds):
            a, b, c, f = sums[4 * e : 4 * e + 4]
            pacc[d * cpd : (d + 1) * cpd, :tb] = a + jnp.where(edge, 0.0, b)
            pacc[d * cpd : (d + 1) * cpd, tb:] = jnp.where(edge, b, c - f)
    signs = jnp.concatenate([parity, parity], axis=1)
    seg_spec = jnp.concatenate(
        [pacc[s * cpd : (s + 1) * cpd, :] + signs * pacc[(s + 1) * cpd : (s + 2) * cpd, :] for s in range(nz)], axis=0
    )
    tap_grad = from_spectrum(seg_spec)

    spots = jnp.concatenate([tap_grad] * rr, axis=0)
    spots = jnp.where(iota((lanes, tb), 1) % rr == iota((lanes, tb), 0) // half, spots, 0.0)
    owner = (iota((n, tb), 1) // rr == iota((n, tb), 0)).astype(BF16)
    vs[:, 0, :] = dot(jnp.concatenate([owner, owner], axis=1), jnp.concatenate(halves(spots), axis=1), 1, 1)
    for peer in peers:
        send(vs.at[peer], vr.at[ctx], vsend, vrecv, (peer, z))
    vr[pl.ds(ctx, 1)] = vs[pl.ds(ctx, 1)]

    wait_all(tr, trecv)
    placed = dot(tr[:, 0, :].T.astype(BF16), owner, 1, 0)
    placed = jnp.where(iota((lanes, tb), 1) % rr == iota((lanes, tb), 0) // half, placed, 0.0)
    own_taps = placed[:half]
    for r in range(1, rr):
        own_taps = own_taps + placed[r * half : (r + 1) * half]

    kt[...] = to_spectrum(own_taps.astype(BF16))
    kernels = []
    for d in range(nz + 1):
        real = imag = jnp.zeros((cpd, tb), F32)
        if d < nz:
            real, imag = kt[d * cpd : (d + 1) * cpd, :tb], kt[d * cpd : (d + 1) * cpd, tb:]
        if d > 0:
            real = real + parity * kt[(d - 1) * cpd : d * cpd, :tb]
            imag = imag + parity * kt[(d - 1) * cpd : d * cpd, tb:]
        kernels.append((real, jnp.where(edge, 0.0, imag), jnp.where(edge, imag, real)))

    def step(i, carry):
        zero = jnp.zeros((cpd, tb), F32)
        real, imag = [zero] * 4, [zero] * 4
        for at in range(nz + 4):
            gr, gi = spec_at(i * 4 + at, 0)
            for j in range(4):
                if 0 <= at - j <= nz:
                    k1, k2, k3 = kernels[at - j]
                    real[j] += k1 * gr + k2 * gi
                    imag[j] += k3 * gi - k2 * gr
        for j in range(4):
            at = pl.ds(pl.multiple_of((i * 4 + j) * cpd, cpd), cpd)
            ys[at, :tb] = real[j]
            ys[at, tb:] = imag[j]
        return carry

    lax.fori_loop(0, n // 4, step, 0)
    o1[...] = from_spectrum(ys[...]).astype(BF16).reshape(n, cpd, tb)

    for peer in peers:
        send(o1.at[peer], q2.at[ctx], qsend, qrecv, (peer, z))
    q2[pl.ds(ctx, 1)] = o1[pl.ds(ctx, 1)]

    wait_all(vr, vrecv)
    group2 = jnp.concatenate([group, group], axis=0).astype(BF16)
    picked = dot(jnp.concatenate(halves(vr[:, 0, :].T), axis=1), group2, 1, 0)
    picked = jnp.where(own_channel, picked, 0.0).reshape(rr, nz, cpd, width)
    tap_rows = jnp.sum(picked, axis=2)
    for q in range(q_tiles):
        for r in range(rr):
            s3[pl.ds(r * q_tiles + q, nz, stride=tile), :] = tap_rows[r, :, q * tb : (q + 1) * tb]
    vzc = []
    for k in range(1, nz):
        vzc.append(send(rows(s3, z_peers[k], tile), rows(o3, z, tile), vzsend.at[k], vzrecv.at[k], (ctx, z_peers[k])))
    o3[pl.ds(pl.multiple_of(z * tile, tile), tile), :] = s3[pl.ds(pl.multiple_of(z * tile, tile), tile), :]

    wait_all(q2, qrecv)
    out_ref[...] = q2[...].astype(F32).reshape(width, tb).T.astype(BF16)

    for copy in vzc:
        copy.wait_recv()
    for src in range(nz):
        for r in range(rr):
            for q in range(q_tiles):
                at = src * width + q * tb
                row = src * tile + r * q_tiles + q
                tg_ref[r, :, at : at + tb] = o3[row : row + 1, :]

    for copy in zc + vzc:
        copy.wait_send()
    for ref, sem in ((s1, xsend), (ts, tsend), (vs, vsend), (o1, qsend)):
        wait_all(ref, sem)


def shards(grad_out, inputs, filter_taps):
    tb, width = grad_out.shape
    n = lax.axis_size("ctx")
    nz = lax.axis_size("ch")
    nu = math.isqrt(n)
    ny = n // nu
    nc = 2
    nx = nu // nc
    rr = filter_taps.shape[0]
    cpd = width // n
    tile = rr * width // tb
    lanes = rr * cpd * nz
    vmem = pltpu.VMEM
    dma = pltpu.SemaphoreType.DMA
    return pl.pallas_call(
        functools.partial(kernel, (n, ny, nx, nc, nz, tb, cpd, rr)),
        out_shape=(
            pltpu.VMEM((tb, width), BF16),
            pltpu.VMEM((rr, 1, nz * width), F32),
        ),
        in_specs=[pl.BlockSpec(memory_space=pl.ANY)] * 5,
        out_specs=[pl.BlockSpec(memory_space=vmem)] * 2,
        scratch_shapes=[
            vmem((tb, width), BF16),
            vmem((tb, width), BF16),
            vmem((rr, nz * width), BF16),
            vmem((2 * tb, 2 * tb), BF16),
            vmem((6 * tb, tb), BF16),
            vmem((n, 2 * cpd, tb), BF16),
            vmem((n, 2 * cpd, tb), BF16),
            vmem(((n + nz) * 2 * cpd, 2 * tb), F32),
            vmem((nz * tile, tb), F32),
            vmem((nz * tile, tb), F32),
            vmem((n, 1, lanes), F32),
            vmem((n, 1, lanes), F32),
            vmem((cpd * (nz + 1), 2 * tb), F32),
            vmem((cpd * nz, 2 * tb), F32),
            vmem((n, 1, lanes), F32),
            vmem((n, 1, lanes), F32),
            vmem((nz * tile, tb), F32),
            vmem((nz * tile, tb), F32),
            vmem((n * cpd, 2 * tb), F32),
            vmem((n, cpd, tb), BF16),
            vmem((n, cpd, tb), BF16),
            dma((5,)), dma, dma, dma((nz,)), dma((nz,)), dma, dma, dma, dma, dma((nz,)), dma((nz,)), dma, dma,
        ],
        compiler_params=pltpu.CompilerParams(collective_id=0, has_side_effects=True),
    )(grad_out, inputs, filter_taps.reshape(rr, nz * width), *dft_tables(tb))


def solution(mesh):
    placed = (P("ctx", "ch"), P("ctx", "ch"), P("ctx", "ch", None))
    return jax.shard_map(
        shards,
        mesh=mesh,
        in_specs=placed,
        out_specs=(P("ctx", "ch"), P("ctx", "ch", None)),
        check_vma=False,
    )
```

```python
import functools
import math

import jax
import jax.numpy as jnp
import numpy as np
from jax import lax
from jax.experimental import pallas as pl
from jax.experimental.pallas import tpu as pltpu
from jax.sharding import PartitionSpec as P

MESH = pl.DeviceIdType.MESH
F32 = jnp.float32
BF16 = jnp.bfloat16
EXACT = lax.Precision.HIGHEST


def iota(shape, axis):
    return lax.broadcasted_iota(jnp.int32, shape, axis)


def dot(a, b, ca, cb, precision=None):
    return lax.dot_general(
        a, b, (((ca,), (cb,)), ((), ())), precision=precision, preferred_element_type=F32
    )


def halves(v):
    upper = v.astype(BF16)
    return upper, (v - upper.astype(F32)).astype(BF16)


def dft_tables(tb):
    place = np.arange(tb)[:, None]
    freq = np.arange(tb)[None, :]
    angle = (place * freq % (2 * tb)) * (np.pi / tb)
    parity = np.where(place % 2 == 0, 1.0, -1.0)
    forward = np.concatenate([np.cos(angle), np.where(freq == 0, parity, -np.sin(angle))], axis=1)
    weight = np.where(np.arange(2 * tb) % tb == 0, 0.5, 1.0) / tb
    backward = (forward * weight).T

    def split(table):
        table = table.astype(np.float32)
        upper = table.astype(BF16)
        return upper, (table - upper.astype(np.float32)).astype(BF16)

    fu, fl = split(forward)
    bu, bl = split(backward)
    return np.concatenate([fu, fl], axis=0), np.concatenate([bu, bu, bl], axis=0)


def kernel(
    dims, g_hbm, x_hbm, f_hbm, fwd_hbm, inv_hbm, out_ref, tg_ref,
    gv, xv, fv, fwd, inv, s1, r2, sp,
    s0, t1, ts, tr,
    pacc, kt, vs, vr, s3, o3,
    ys, o1, q2,
    insem, xsend, xrecv, zsend, zrecv, tsend, trecv, vsend, vrecv, vzsend, vzrecv, qsend, qrecv,
):
    n, ny, nx, nc, nz, tb, cpd, rr = dims
    nu = nx * nc
    width = cpd * n
    q_tiles = width // tb
    lanes = rr * cpd * nz
    tile = rr * q_tiles
    pair = 2 * cpd
    half = cpd * nz

    ctx = lax.axis_index("ctx")
    z = lax.axis_index("ch")
    y = lax.div(ctx, nu)
    x = lax.rem(lax.div(ctx, nc), nx)
    core = lax.rem(ctx, nc)

    def hops(offset):
        dy, dx, _ = offset
        return min(dy, ny - dy) + min(dx, nx - dx)

    offsets = [(dy, dx, dc) for dc in range(nc) for dx in range(nx) for dy in range(ny)][1:]
    offsets.sort(key=lambda o: -hops(o))
    y_rows = [lax.rem(y + d, ny) for d in range(ny)]
    y_at = [row * nu for row in y_rows]
    x_at = [lax.rem(x + d, nx) * nc for d in range(nx)]
    c_at = [lax.rem(core + d, nc) for d in range(nc)]
    u_at = {(dx, dc): x_at[dx] + c_at[dc] for dx in range(nx) for dc in range(nc)}
    peers = [y_at[dy] + u_at[dx, dc] for dy, dx, dc in offsets]
    z_peers = [lax.rem(z + k, nz) for k in range(nz)]

    barrier = pltpu.get_barrier_semaphore()
    for peer in peers:
        pl.semaphore_signal(barrier, inc=1, device_id=(peer, z), device_id_type=MESH)
    for k in range(1, nz):
        pl.semaphore_signal(barrier, inc=1, device_id=(ctx, z_peers[k]), device_id_type=MESH)

    loads = [
        pltpu.make_async_copy(f_hbm, fv, insem.at[2]),
        pltpu.make_async_copy(g_hbm, gv, insem.at[0]),
        pltpu.make_async_copy(x_hbm, xv, insem.at[1]),
        pltpu.make_async_copy(fwd_hbm, fwd, insem.at[3]),
        pltpu.make_async_copy(inv_hbm, inv, insem.at[4]),
    ]
    for load in loads:
        load.start()

    def send(src, dst, ssem, rsem, device):
        copy = pltpu.make_async_remote_copy(
            src_ref=src, dst_ref=dst, send_sem=ssem, recv_sem=rsem,
            device_id=device, device_id_type=MESH,
        )
        copy.start()
        return copy

    def rows(ref, index, count):
        return ref.at[pl.ds(pl.multiple_of(index * count, count), count)]

    def wait_all(ref, sem):
        pltpu.make_async_copy(ref.at[pl.ds(0, n - 1)], ref.at[pl.ds(0, n - 1)], sem).wait()

    loads[0].wait()
    taps_in = fv[...].astype(F32)
    for to in range(nz):
        for r in range(rr):
            for q in range(q_tiles):
                at = to * width + q * tb
                s0[to * tile + r * q_tiles + q : to * tile + r * q_tiles + q + 1, :] = taps_in[r : r + 1, at : at + tb]

    loads[1].wait()
    loads[2].wait()
    g_t = gv[...].astype(F32).T.reshape(n, cpd, tb)
    x_t = xv[...].astype(F32).T.reshape(n, cpd, tb)
    s1[...] = jnp.concatenate([g_t, x_t], axis=1).astype(BF16)
    sp[n * pair :, :] = jnp.zeros((nz * pair, 2 * tb), F32)

    pl.semaphore_wait(barrier, n - 1 + nz - 1)

    zc = []
    for k in range(1, nz):
        zc.append(send(rows(s0, z_peers[k], tile), rows(t1, z, tile), zsend.at[k], zrecv.at[k], (ctx, z_peers[k])))
    for peer in peers:
        send(s1.at[peer], r2.at[ctx], xsend, xrecv.at[y], (peer, z))
    r2[pl.ds(ctx, 1)] = s1[pl.ds(ctx, 1)]
    t1[pl.ds(pl.multiple_of(z * tile, tile), tile), :] = s0[pl.ds(pl.multiple_of(z * tile, tile), tile), :]

    for copy in zc:
        copy.wait_recv()
    taps = jnp.concatenate([t1[pl.ds(q, nz * rr, stride=q_tiles), :] for q in range(q_tiles)], axis=1)
    lane_r = iota((lanes, nz * rr), 0) // half
    lane_s = iota((lanes, nz * rr), 0) % half // cpd
    spread = (iota((lanes, nz * rr), 1) == lane_s * rr + lane_r).astype(BF16)
    own_channel = iota((lanes, width), 0) % cpd == iota((lanes, width), 1) % cpd
    group = iota((n, width), 0) == iota((n, width), 1) // cpd
    spread_taps = jnp.where(own_channel, dot(spread, taps.astype(BF16), 1, 0), 0.0)
    ts[:, 0, :] = dot(group.astype(BF16), spread_taps.astype(BF16), 1, 1)
    for peer in peers:
        send(ts.at[peer], tr.at[ctx], tsend, trecv, (peer, z))
    tr[pl.ds(ctx, 1)] = ts[pl.ds(ctx, 1)]

    def to_spectrum(v):
        return dot(jnp.concatenate([v, v], axis=1), fwd[...], 1, 0)

    def from_spectrum(v):
        upper, lower = halves(v)
        return dot(jnp.concatenate([upper, lower, upper], axis=1), inv[...], 1, 0)

    loads[3].wait()
    loads[4].wait()
    lane = iota((cpd, tb), 1)
    parity = jnp.where(lane % 2 == 0, 1.0, -1.0)
    edge = lane == 0
    zero = jnp.zeros((cpd, tb), F32)

    def spec_at(block, first):
        at = pl.ds(pl.multiple_of(block * pair + first, cpd), cpd)
        return sp[at, :tb], sp[at, tb:]

    def take_row(k):
        row = y_rows[k]
        count = nu - 1 if k == 0 else nu
        pltpu.make_async_copy(r2.at[pl.ds(0, count)], r2.at[pl.ds(0, count)], xrecv.at[row]).wait()
        blocks = r2[pl.ds(row * nu, nu)].reshape(nu * pair, tb)
        sp[pl.ds(pl.multiple_of(row * nu * pair, nu * pair), nu * pair), :] = to_spectrum(blocks)

    def add_row(k, first):
        start = y_rows[k] * nu
        for d0 in range(0, nz + 1, 3):
            ds = range(d0, min(d0 + 3, nz + 1))
            if first:
                sums = [zero] * (4 * len(ds))
            else:
                sums = [pacc[4 * d + e] for d in ds for e in range(4)]
            for i in range(0, nu, span):
                xs = [spec_at(start + i + j, cpd) for j in range(span)]
                for at in range(ds[0], ds[-1] + span):
                    gr, gi = spec_at(start + i + at, 0)
                    for e, d in enumerate(ds):
                        if 0 <= at - d < span:
                            xr, xi = xs[at - d]
                            sums[4 * e] += xr * gr
                            sums[4 * e + 1] += xi * gi
                            sums[4 * e + 2] += xr * gi
                            sums[4 * e + 3] += xi * gr
            for e, d in enumerate(ds):
                for part in range(4):
                    pacc[4 * d + part] = sums[4 * e + part]

    span = min(4, nu)
    far_first = sorted(range(ny), key=lambda k: -min(k, ny - k))
    taken = set()
    added = set()
    for k in [0] + [k for k in far_first if k]:
        take_row(k)
        taken.add(k)
        for prev in range(ny):
            if prev not in added and prev in taken and (prev + 1) % ny in taken:
                add_row(prev, not added)
                added.add(prev)

    def lag(d):
        a, b, c, f = [pacc[4 * d + e] for e in range(4)]
        return jnp.concatenate([a + jnp.where(edge, 0.0, b), jnp.where(edge, b, c - f)], axis=1)

    lags = [lag(d) for d in range(nz + 1)]
    signs = jnp.concatenate([parity, parity], axis=1)
    seg_spec = jnp.concatenate([lags[s] + signs * lags[s + 1] for s in range(nz)], axis=0)
    tap_grad = from_spectrum(seg_spec)

    spots = jnp.concatenate([tap_grad] * rr, axis=0)
    spots = jnp.where(iota((lanes, tb), 1) % rr == iota((lanes, tb), 0) // half, spots, 0.0)
    owner = (iota((n, tb), 1) // rr == iota((n, tb), 0)).astype(BF16)
    vs[:, 0, :] = dot(jnp.concatenate([owner, owner], axis=1), jnp.concatenate(halves(spots), axis=1), 1, 1)
    for peer in peers:
        send(vs.at[peer], vr.at[ctx], vsend, vrecv, (peer, z))
    vr[pl.ds(ctx, 1)] = vs[pl.ds(ctx, 1)]

    wait_all(tr, trecv)
    placed = dot(tr[:, 0, :].T.astype(BF16), owner, 1, 0)
    placed = jnp.where(iota((lanes, tb), 1) % rr == iota((lanes, tb), 0) // half, placed, 0.0)
    own_taps = placed[:half]
    for r in range(1, rr):
        own_taps = own_taps + placed[r * half : (r + 1) * half]

    kt[...] = to_spectrum(own_taps.astype(BF16))
    kernels = []
    for d in range(nz + 1):
        real = imag = jnp.zeros((cpd, tb), F32)
        if d < nz:
            real, imag = kt[d * cpd : (d + 1) * cpd, :tb], kt[d * cpd : (d + 1) * cpd, tb:]
        if d > 0:
            real = real + parity * kt[(d - 1) * cpd : d * cpd, :tb]
            imag = imag + parity * kt[(d - 1) * cpd : d * cpd, tb:]
        kernels.append((real, jnp.where(edge, 0.0, imag), jnp.where(edge, imag, real)))

    for pick in range(0, ny, 2):
        chunk = far_first[pick : pick + 2]
        for half_at, k in enumerate(chunk):
            start = y_rows[k] * nu
            for i in range(0, nu, span):
                real, imag = [zero] * span, [zero] * span
                for at in range(nz + span):
                    gr, gi = spec_at(start + i + at, 0)
                    for j in range(span):
                        if 0 <= at - j <= nz:
                            k1, k2, k3 = kernels[at - j]
                            real[j] += k1 * gr + k2 * gi
                            imag[j] += k3 * gi - k2 * gr
                for j in range(span):
                    at = (half_at * nu + i + j) * cpd
                    ys[at : at + cpd, :tb] = real[j]
                    ys[at : at + cpd, tb:] = imag[j]
        outs = from_spectrum(ys[...]).astype(BF16).reshape(len(chunk), nu, cpd, tb)
        for half_at, k in enumerate(chunk):
            o1[pl.ds(y_rows[k] * nu, nu)] = outs[half_at]
        for dy, dx, dc in offsets:
            if dy in chunk:
                peer = y_at[dy] + u_at[dx, dc]
                send(o1.at[peer], q2.at[ctx], qsend, qrecv, (peer, z))
    q2[pl.ds(ctx, 1)] = o1[pl.ds(ctx, 1)]

    wait_all(vr, vrecv)
    group2 = jnp.concatenate([group, group], axis=0).astype(BF16)
    picked = dot(jnp.concatenate(halves(vr[:, 0, :].T), axis=1), group2, 1, 0)
    picked = jnp.where(own_channel, picked, 0.0).reshape(rr, nz, cpd, width)
    tap_rows = jnp.sum(picked, axis=2)
    for q in range(q_tiles):
        for r in range(rr):
            s3[pl.ds(r * q_tiles + q, nz, stride=tile), :] = tap_rows[r, :, q * tb : (q + 1) * tb]
    vzc = []
    for k in range(1, nz):
        vzc.append(send(rows(s3, z_peers[k], tile), rows(o3, z, tile), vzsend.at[k], vzrecv.at[k], (ctx, z_peers[k])))
    o3[pl.ds(pl.multiple_of(z * tile, tile), tile), :] = s3[pl.ds(pl.multiple_of(z * tile, tile), tile), :]

    wait_all(q2, qrecv)
    out_ref[...] = q2[...].astype(F32).reshape(width, tb).T.astype(BF16)

    for copy in vzc:
        copy.wait_recv()
    for src in range(nz):
        for r in range(rr):
            for q in range(q_tiles):
                at = src * width + q * tb
                row = src * tile + r * q_tiles + q
                tg_ref[r, :, at : at + tb] = o3[row : row + 1, :]

    for copy in zc + vzc:
        copy.wait_send()
    for ref, sem in ((s1, xsend), (ts, tsend), (vs, vsend), (o1, qsend)):
        wait_all(ref, sem)


def write_out(a_ref, b_ref, a_out, b_out, sem):
    copies = [pltpu.make_async_copy(a_ref, a_out, sem.at[0]), pltpu.make_async_copy(b_ref, b_out, sem.at[1])]
    for copy in copies:
        copy.start()
    for copy in copies:
        copy.wait()


def shards(grad_out, inputs, filter_taps):
    tb, width = grad_out.shape
    n = lax.axis_size("ctx")
    nz = lax.axis_size("ch")
    nu = math.isqrt(n)
    ny = n // nu
    nc = 2
    nx = nu // nc
    rr = filter_taps.shape[0]
    cpd = width // n
    tile = rr * width // tb
    lanes = rr * cpd * nz
    vmem = pltpu.VMEM
    dma = pltpu.SemaphoreType.DMA
    results = pl.pallas_call(
        functools.partial(kernel, (n, ny, nx, nc, nz, tb, cpd, rr)),
        out_shape=(
            pltpu.VMEM((tb, width), BF16),
            pltpu.VMEM((rr, 1, nz * width), F32),
        ),
        in_specs=[pl.BlockSpec(memory_space=pl.ANY)] * 5,
        out_specs=[pl.BlockSpec(memory_space=vmem)] * 2,
        scratch_shapes=[
            vmem((tb, width), BF16),
            vmem((tb, width), BF16),
            vmem((rr, nz * width), BF16),
            vmem((2 * tb, 2 * tb), BF16),
            vmem((6 * tb, tb), BF16),
            vmem((n, 2 * cpd, tb), BF16),
            vmem((n, 2 * cpd, tb), BF16),
            vmem(((n + nz) * 2 * cpd, 2 * tb), F32),
            vmem((nz * tile, tb), F32),
            vmem((nz * tile, tb), F32),
            vmem((n, 1, lanes), F32),
            vmem((n, 1, lanes), F32),
            vmem((4 * (nz + 1), cpd, tb), F32),
            vmem((cpd * nz, 2 * tb), F32),
            vmem((n, 1, lanes), F32),
            vmem((n, 1, lanes), F32),
            vmem((nz * tile, tb), F32),
            vmem((nz * tile, tb), F32),
            vmem((2 * nu * cpd, 2 * tb), F32),
            vmem((n, cpd, tb), BF16),
            vmem((n, cpd, tb), BF16),
            dma((5,)), dma, dma((ny,)), dma((nz,)), dma((nz,)), dma, dma, dma, dma, dma((nz,)), dma((nz,)), dma, dma,
        ],
        compiler_params=pltpu.CompilerParams(collective_id=0, has_side_effects=True),
    )(grad_out, inputs, filter_taps.reshape(rr, nz * width), *dft_tables(tb))
    return pl.pallas_call(
        write_out,
        out_shape=[jax.ShapeDtypeStruct(r.shape, r.dtype) for r in results],
        in_specs=[pl.BlockSpec(memory_space=vmem)] * 2,
        out_specs=[pl.BlockSpec(memory_space=pl.ANY)] * 2,
        scratch_shapes=[dma((2,))],
    )(*[pltpu.with_memory_space_constraint(r, vmem) for r in results])


def solution(mesh):
    placed = (P("ctx", "ch"), P("ctx", "ch"), P("ctx", "ch", None))
    return jax.shard_map(
        shards,
        mesh=mesh,
        in_specs=placed,
        out_specs=(P("ctx", "ch"), P("ctx", "ch", None)),
        check_vma=False,
    )
```

```python
import functools
import math

import jax
import jax.numpy as jnp
import numpy as np
from jax import lax
from jax.experimental import pallas as pl
from jax.experimental.pallas import tpu as pltpu
from jax.sharding import PartitionSpec as P

MESH = pl.DeviceIdType.MESH
F32 = jnp.float32
BF16 = jnp.bfloat16


def iota(shape, axis):
    return lax.broadcasted_iota(jnp.int32, shape, axis)


def dot(a, b, ca, cb):
    return lax.dot_general(a, b, (((ca,), (cb,)), ((), ())), preferred_element_type=F32)


def halves(v):
    upper = v.astype(BF16)
    return upper, (v - upper.astype(F32)).astype(BF16)


def dft_tables(tb, rr):
    place = np.arange(tb)[:, None]
    freq = np.arange(tb)[None, :]
    angle = (place * freq % (2 * tb)) * (np.pi / tb)
    parity = np.where(place % 2 == 0, 1.0, -1.0)
    forward = np.concatenate([np.cos(angle), np.where(freq == 0, parity, -np.sin(angle))], axis=1)
    weight = np.where(np.arange(2 * tb) % tb == 0, 0.5, 1.0) / tb
    backward = (forward * weight).T

    def split(table):
        table = table.astype(np.float32)
        upper = table.astype(BF16)
        return upper, (table - upper.astype(np.float32)).astype(BF16)

    fu, fl = split(forward)
    bu, bl = split(backward)
    inverse = np.concatenate([bu, bu, bl], axis=0)
    by_owner = inverse.T.reshape(tb // rr, rr, 6 * tb).transpose(1, 0, 2).reshape(tb, 6 * tb)
    return np.concatenate([fu, fl], axis=0), inverse, by_owner


def kernel(
    dims, g_hbm, x_hbm, f_hbm, fwd_hbm, inv_hbm, own_hbm, out_ref, tg_ref,
    gv, xv, fv, fwd, inv, own_inv, gt, xt, s1, r2, sp,
    s0, t1, ts, tr,
    pacc, kt, vs, vr, vt, s3, o3,
    ys, o1, q2,
    insem, xsend, xrecv, zsend, zrecv, tsend, trecv, vsend, vrecv, vzsend, vzrecv, qsend, qrecv,
):
    n, ny, nx, nc, nz, tb, cpd, rr = dims
    nu = nx * nc
    width = cpd * n
    q_tiles = width // tb
    lanes = rr * cpd * nz
    tile = rr * q_tiles
    pair = 2 * cpd
    half = cpd * nz

    ctx = lax.axis_index("ctx")
    z = lax.axis_index("ch")
    y = lax.div(ctx, nu)
    x = lax.rem(lax.div(ctx, nc), nx)
    core = lax.rem(ctx, nc)

    def hops(offset):
        dy, dx, _ = offset
        return min(dy, ny - dy) + min(dx, nx - dx)

    offsets = [(dy, dx, dc) for dc in range(nc) for dx in range(nx) for dy in range(ny)][1:]
    offsets.sort(key=lambda o: -hops(o))
    y_rows = [lax.rem(y + d, ny) for d in range(ny)]
    y_at = [row * nu for row in y_rows]
    x_at = [lax.rem(x + d, nx) * nc for d in range(nx)]
    c_at = [lax.rem(core + d, nc) for d in range(nc)]
    u_at = {(dx, dc): x_at[dx] + c_at[dc] for dx in range(nx) for dc in range(nc)}
    peers = [y_at[dy] + u_at[dx, dc] for dy, dx, dc in offsets]
    z_peers = [lax.rem(z + k, nz) for k in range(nz)]

    barrier = pltpu.get_barrier_semaphore()
    for peer in peers:
        pl.semaphore_signal(barrier, inc=1, device_id=(peer, z), device_id_type=MESH)
    for k in range(1, nz):
        pl.semaphore_signal(barrier, inc=1, device_id=(ctx, z_peers[k]), device_id_type=MESH)

    loads = [
        pltpu.make_async_copy(f_hbm, fv, insem.at[2]),
        pltpu.make_async_copy(g_hbm, gv, insem.at[0]),
        pltpu.make_async_copy(x_hbm, xv, insem.at[1]),
        pltpu.make_async_copy(fwd_hbm, fwd, insem.at[3]),
        pltpu.make_async_copy(inv_hbm, inv, insem.at[4]),
        pltpu.make_async_copy(own_hbm, own_inv, insem.at[5]),
    ]
    for load in loads:
        load.start()

    def send(src, dst, ssem, rsem, device):
        copy = pltpu.make_async_remote_copy(
            src_ref=src, dst_ref=dst, send_sem=ssem, recv_sem=rsem,
            device_id=device, device_id_type=MESH,
        )
        copy.start()
        return copy

    def rows(ref, index, count):
        return ref.at[pl.ds(pl.multiple_of(index * count, count), count)]

    def wait_all(ref, sem):
        pltpu.make_async_copy(ref.at[pl.ds(0, n - 1)], ref.at[pl.ds(0, n - 1)], sem).wait()

    def wait_z(ref, sem):
        part = ref.at[pl.ds(0, (nz - 1) * tile)]
        pltpu.make_async_copy(part, part, sem).wait()

    loads[0].wait()
    taps_in = fv[...].astype(F32)
    for to in range(nz):
        for r in range(rr):
            for q in range(q_tiles):
                at = to * width + q * tb
                s0[to * tile + r * q_tiles + q : to * tile + r * q_tiles + q + 1, :] = taps_in[r : r + 1, at : at + tb]

    loads[1].wait()
    loads[2].wait()
    gt[...] = gv[...].astype(F32).T
    xt[...] = xv[...].astype(F32).T
    for j in range(n):
        own = pl.ds(j, cpd, stride=n)
        s1[j] = jnp.concatenate([gt[own, :], xt[own, :]], axis=0).astype(BF16)
    sp[n * pair :, :] = jnp.zeros((nz * pair, 2 * tb), F32)

    pl.semaphore_wait(barrier, n - 1 + nz - 1)

    for k in range(1, nz):
        send(rows(s0, z_peers[k], tile), rows(t1, z, tile), zsend, zrecv, (ctx, z_peers[k]))
    for peer in peers:
        send(s1.at[peer], r2.at[ctx], xsend, xrecv.at[y], (peer, z))
    r2[pl.ds(ctx, 1)] = s1[pl.ds(ctx, 1)]
    t1[pl.ds(pl.multiple_of(z * tile, tile), tile), :] = s0[pl.ds(pl.multiple_of(z * tile, tile), tile), :]

    wait_z(t1, zrecv)
    taps = jnp.concatenate([t1[pl.ds(q, nz * rr, stride=q_tiles), :] for q in range(q_tiles)], axis=1)
    lane_r = iota((lanes, nz * rr), 0) // half
    lane_s = iota((lanes, nz * rr), 0) % half // cpd
    spread = (iota((lanes, nz * rr), 1) == lane_s * rr + lane_r).astype(BF16)
    own_channel = iota((lanes, width), 0) % cpd == iota((lanes, width), 1) // n
    group = iota((n, width), 0) == iota((n, width), 1) % n
    spread_taps = jnp.where(own_channel, dot(spread, taps.astype(BF16), 1, 0), 0.0)
    ts[:, 0, :] = dot(group.astype(BF16), spread_taps.astype(BF16), 1, 1)
    for peer in peers:
        send(ts.at[peer], tr.at[ctx], tsend, trecv, (peer, z))
    tr[pl.ds(ctx, 1)] = ts[pl.ds(ctx, 1)]

    def to_spectrum(v):
        return dot(jnp.concatenate([v, v], axis=1), fwd[...], 1, 0)

    def thirds(v):
        upper, lower = halves(v)
        return jnp.concatenate([upper, lower, upper], axis=1)

    def from_spectrum(v):
        return dot(thirds(v), inv[...], 1, 0)

    loads[3].wait()
    loads[4].wait()
    loads[5].wait()
    lane = iota((cpd, tb), 1)
    parity = jnp.where(lane % 2 == 0, 1.0, -1.0)
    edge = lane == 0
    zero = jnp.zeros((cpd, tb), F32)

    def spec_at(block, first):
        at = pl.ds(pl.multiple_of(block * pair + first, cpd), cpd)
        return sp[at, :tb], sp[at, tb:]

    def take_row(k):
        row = y_rows[k]
        count = nu - 1 if k == 0 else nu
        pltpu.make_async_copy(r2.at[pl.ds(0, count)], r2.at[pl.ds(0, count)], xrecv.at[row]).wait()
        blocks = r2[pl.ds(row * nu, nu)].reshape(nu * pair, tb)
        sp[pl.ds(pl.multiple_of(row * nu * pair, nu * pair), nu * pair), :] = to_spectrum(blocks)

    def add_row(k, first):
        start = y_rows[k] * nu
        for d0 in range(0, nz + 1, 3):
            ds = range(d0, min(d0 + 3, nz + 1))
            if first:
                sums = [zero] * (4 * len(ds))
            else:
                sums = [pacc[4 * d + e] for d in ds for e in range(4)]
            for i in range(0, nu, span):
                xs = [spec_at(start + i + j, cpd) for j in range(span)]
                for at in range(ds[0], ds[-1] + span):
                    gr, gi = spec_at(start + i + at, 0)
                    for e, d in enumerate(ds):
                        if 0 <= at - d < span:
                            xr, xi = xs[at - d]
                            sums[4 * e] += xr * gr
                            sums[4 * e + 1] += xi * gi
                            sums[4 * e + 2] += xr * gi
                            sums[4 * e + 3] += xi * gr
            for e, d in enumerate(ds):
                for part in range(4):
                    pacc[4 * d + part] = sums[4 * e + part]

    span = min(4, nu)
    far_first = sorted(range(ny), key=lambda k: (-min(k, ny - k), -k))
    taken = set()
    added = set()
    for k in [0] + [k for k in far_first if k]:
        take_row(k)
        taken.add(k)
        for prev in range(ny):
            if prev not in added and prev in taken and (prev + 1) % ny in taken:
                add_row(prev, not added)
                added.add(prev)

    def lag(d):
        a, b, c, f = [pacc[4 * d + e] for e in range(4)]
        return jnp.concatenate([a + jnp.where(edge, 0.0, b), jnp.where(edge, b, c - f)], axis=1)

    lags = [lag(d) for d in range(nz + 1)]
    signs = jnp.concatenate([parity, parity], axis=1)
    seg_spec = jnp.concatenate([lags[s] + signs * lags[s + 1] for s in range(nz)], axis=0)
    by_owner = dot(own_inv[...], thirds(seg_spec), 1, 1)
    vs[:, 0, :] = jnp.concatenate([by_owner[r * n : (r + 1) * n] for r in range(rr)], axis=1)
    for peer in peers:
        send(vs.at[peer], vr.at[ctx], vsend, vrecv, (peer, z))
    vr[pl.ds(ctx, 1)] = vs[pl.ds(ctx, 1)]

    wait_all(tr, trecv)
    owner = (iota((n, tb), 1) // rr == iota((n, tb), 0)).astype(BF16)
    placed = dot(tr[:, 0, :].T.astype(BF16), owner, 1, 0)
    placed = jnp.where(iota((lanes, tb), 1) % rr == iota((lanes, tb), 0) // half, placed, 0.0)
    own_taps = placed[:half]
    for r in range(1, rr):
        own_taps = own_taps + placed[r * half : (r + 1) * half]

    kt[...] = to_spectrum(own_taps.astype(BF16))
    kernels = []
    for d in range(nz + 1):
        real = imag = jnp.zeros((cpd, tb), F32)
        if d < nz:
            real, imag = kt[d * cpd : (d + 1) * cpd, :tb], kt[d * cpd : (d + 1) * cpd, tb:]
        if d > 0:
            real = real + parity * kt[(d - 1) * cpd : d * cpd, :tb]
            imag = imag + parity * kt[(d - 1) * cpd : d * cpd, tb:]
        kernels.append((real, jnp.where(edge, 0.0, imag), jnp.where(edge, imag, real)))

    for pick in range(0, ny, 2):
        chunk = far_first[pick : pick + 2]
        for half_at, k in enumerate(chunk):
            start = y_rows[k] * nu
            for i in range(0, nu, span):
                real, imag = [zero] * span, [zero] * span
                for at in range(nz + span):
                    gr, gi = spec_at(start + i + at, 0)
                    for j in range(span):
                        if 0 <= at - j <= nz:
                            k1, k2, k3 = kernels[at - j]
                            real[j] += k1 * gr + k2 * gi
                            imag[j] += k3 * gi - k2 * gr
                for j in range(span):
                    at = (half_at * nu + i + j) * cpd
                    ys[at : at + cpd, :tb] = real[j]
                    ys[at : at + cpd, tb:] = imag[j]
        outs = from_spectrum(ys[...]).astype(BF16).reshape(len(chunk), nu, cpd, tb)
        for half_at, k in enumerate(chunk):
            o1[pl.ds(y_rows[k] * nu, nu)] = outs[half_at]
        for dy, dx, dc in offsets:
            if dy in chunk:
                peer = y_at[dy] + u_at[dx, dc]
                send(o1.at[peer], q2.at[ctx], qsend, qrecv, (peer, z))
    q2[pl.ds(ctx, 1)] = o1[pl.ds(ctx, 1)]

    wait_all(vr, vrecv)
    vt[...] = vr[:, 0, :].T
    per_tile = tb // n
    for r in range(rr):
        for q in range(q_tiles):
            first = r * half + q * per_tile
            parts = [vt[pl.ds(first + e, nz, stride=cpd), :] for e in range(per_tile)]
            s3[pl.ds(r * q_tiles + q, nz, stride=tile), :] = jnp.concatenate(parts, axis=1)
    for k in range(1, nz):
        send(rows(s3, z_peers[k], tile), rows(o3, z, tile), vzsend, vzrecv, (ctx, z_peers[k]))
    o3[pl.ds(pl.multiple_of(z * tile, tile), tile), :] = s3[pl.ds(pl.multiple_of(z * tile, tile), tile), :]

    wait_all(q2, qrecv)
    for j in range(n):
        gt[pl.ds(j, cpd, stride=n), :] = q2[j].astype(F32)
    out_ref[...] = gt[...].T.astype(BF16)

    wait_z(o3, vzrecv)
    for src in range(nz):
        for r in range(rr):
            for q in range(q_tiles):
                at = src * width + q * tb
                row = src * tile + r * q_tiles + q
                tg_ref[r, :, at : at + tb] = o3[row : row + 1, :]

    wait_z(s0, zsend)
    wait_z(s3, vzsend)
    for ref, sem in ((s1, xsend), (ts, tsend), (vs, vsend), (o1, qsend)):
        wait_all(ref, sem)


def write_out(a_ref, b_ref, a_out, b_out, sem):
    copies = [pltpu.make_async_copy(a_ref, a_out, sem.at[0]), pltpu.make_async_copy(b_ref, b_out, sem.at[1])]
    for copy in copies:
        copy.start()
    for copy in copies:
        copy.wait()


def shards(grad_out, inputs, filter_taps):
    tb, width = grad_out.shape
    n = lax.axis_size("ctx")
    nz = lax.axis_size("ch")
    nu = math.isqrt(n)
    ny = n // nu
    nc = 2
    nx = nu // nc
    rr = filter_taps.shape[0]
    cpd = width // n
    tile = rr * width // tb
    lanes = rr * cpd * nz
    vmem = pltpu.VMEM
    dma = pltpu.SemaphoreType.DMA
    results = pl.pallas_call(
        functools.partial(kernel, (n, ny, nx, nc, nz, tb, cpd, rr)),
        out_shape=(
            pltpu.VMEM((tb, width), BF16),
            pltpu.VMEM((rr, 1, nz * width), F32),
        ),
        in_specs=[pl.BlockSpec(memory_space=pl.ANY)] * 6,
        out_specs=[pl.BlockSpec(memory_space=vmem)] * 2,
        scratch_shapes=[
            vmem((tb, width), BF16),
            vmem((tb, width), BF16),
            vmem((rr, nz * width), BF16),
            vmem((2 * tb, 2 * tb), BF16),
            vmem((6 * tb, tb), BF16),
            vmem((tb, 6 * tb), BF16),
            vmem((width, tb), F32),
            vmem((width, tb), F32),
            vmem((n, 2 * cpd, tb), BF16),
            vmem((n, 2 * cpd, tb), BF16),
            vmem(((n + nz) * 2 * cpd, 2 * tb), F32),
            vmem((nz * tile, tb), F32),
            vmem((nz * tile, tb), F32),
            vmem((n, 1, lanes), F32),
            vmem((n, 1, lanes), F32),
            vmem((4 * (nz + 1), cpd, tb), F32),
            vmem((cpd * nz, 2 * tb), F32),
            vmem((n, 1, lanes), F32),
            vmem((n, 1, lanes), F32),
            vmem((lanes, n), F32),
            vmem((nz * tile, tb), F32),
            vmem((nz * tile, tb), F32),
            vmem((2 * nu * cpd, 2 * tb), F32),
            vmem((n, cpd, tb), BF16),
            vmem((n, cpd, tb), BF16),
            dma((6,)), dma, dma((ny,)), dma, dma, dma, dma, dma, dma, dma, dma, dma, dma,
        ],
        compiler_params=pltpu.CompilerParams(collective_id=0, has_side_effects=True),
    )(grad_out, inputs, filter_taps.reshape(rr, nz * width), *dft_tables(tb, rr))
    return pl.pallas_call(
        write_out,
        out_shape=[jax.ShapeDtypeStruct(r.shape, r.dtype) for r in results],
        in_specs=[pl.BlockSpec(memory_space=vmem)] * 2,
        out_specs=[pl.BlockSpec(memory_space=pl.ANY)] * 2,
        scratch_shapes=[dma((2,))],
    )(*[pltpu.with_memory_space_constraint(r, vmem) for r in results])


def solution(mesh):
    placed = (P("ctx", "ch"), P("ctx", "ch"), P("ctx", "ch", None))
    return jax.shard_map(
        shards,
        mesh=mesh,
        in_specs=placed,
        out_specs=(P("ctx", "ch"), P("ctx", "ch", None)),
        check_vma=False,
    )
```

```python
import functools
import jax
import jax.numpy as jnp
import numpy as np
from jax import lax
from jax.experimental import pallas as pl
from jax.experimental.pallas import tpu as pltpu
from jax.sharding import PartitionSpec as P

MESH = pl.DeviceIdType.MESH
F32 = jnp.float32
BF16 = jnp.bfloat16


def iota(shape, axis):
    return lax.broadcasted_iota(jnp.int32, shape, axis)


def dot(a, b, ca, cb):
    return lax.dot_general(a, b, (((ca,), (cb,)), ((), ())), preferred_element_type=F32)


def halves(v):
    upper = v.astype(BF16)
    return upper, (v - upper.astype(F32)).astype(BF16)


def dft_tables(tb, rr):
    place = np.arange(tb)[:, None]
    freq = np.arange(tb)[None, :]
    angle = (place * freq % (2 * tb)) * (np.pi / tb)
    parity = np.where(place % 2 == 0, 1.0, -1.0)
    forward = np.concatenate([np.cos(angle), np.where(freq == 0, parity, -np.sin(angle))], axis=1)
    weight = np.where(np.arange(2 * tb) % tb == 0, 0.5, 1.0) / tb
    backward = (forward * weight).T

    def split(table):
        table = table.astype(np.float32)
        upper = table.astype(BF16)
        return upper, (table - upper.astype(np.float32)).astype(BF16)

    fu, fl = split(forward)
    bu, bl = split(backward)
    inverse = np.concatenate([bu, bu, bl], axis=0)
    by_owner = inverse.T.reshape(tb // rr, rr, 6 * tb).transpose(1, 0, 2).reshape(tb, 6 * tb)
    return np.concatenate([fu, fl], axis=0), inverse, by_owner


def kernel(
    dims, g_hbm, x_hbm, f_hbm, fwd_hbm, inv_hbm, own_hbm, out_ref, tg_ref,
    gv, xv, fv, fwd, inv, own_inv, gt, xt, sg, sx, rg, rx, pg, px,
    s0, t1, ts, tr,
    pacc, kt, vs, vr, vt, s3, o3,
    ys, o1, q2,
    gates, insem, gsend, grecv, xsend, xrecv, zsend, zrecv, tsend, trecv, vsend, vrecv, vzsend, vzrecv, qsend, qrecv,
):
    n, ny, nx, nc, nz, tb, own, rr = dims
    sub = 8
    nu = nx * nc
    nh = n // 2
    hs = own // sub
    width = own * nh
    q_tiles = width // tb
    lanes = own * nz
    seg = sub * nz
    tile = rr * q_tiles

    ctx = lax.axis_index("ctx")
    z = lax.axis_index("ch")
    y = lax.div(ctx, nu)
    x = lax.rem(lax.div(ctx, nc), nx)
    core = lax.rem(ctx, nc)
    mine = lax.rem(ctx, nh)

    loads = [
        pltpu.make_async_copy(f_hbm, fv, insem.at[2]),
        pltpu.make_async_copy(g_hbm, gv, insem.at[0]),
        pltpu.make_async_copy(x_hbm, xv, insem.at[1]),
        pltpu.make_async_copy(fwd_hbm, fwd, insem.at[3]),
        pltpu.make_async_copy(inv_hbm, inv, insem.at[4]),
        pltpu.make_async_copy(own_hbm, own_inv, insem.at[5]),
    ]
    for load in loads[:3]:
        load.start()

    def hops(offset):
        dy, dx, _ = offset
        return abs(dy) + min(dx, nx - dx)

    offsets = [(dy, dx, dc) for dc in range(nc) for dx in range(nx) for dy in range(-3, 5)]
    offsets = sorted([o for o in offsets if any(o)], key=lambda o: -hops(o))
    near = [o for o in offsets if abs(o[0]) <= 2]
    y_rows = {d: lax.rem(y + d + ny, ny) for d in range(-3, 5)}
    y_at = {d: row * nu for d, row in y_rows.items()}
    x_at = [lax.rem(x + d, nx) * nc for d in range(nx)]
    c_at = [lax.rem(core + d, nc) for d in range(nc)]
    u_at = {(dx, dc): x_at[dx] + c_at[dc] for dx in range(nx) for dc in range(nc)}
    z_peers = [lax.rem(z + k, nz) for k in range(nz)]

    def index_of(offset):
        dy, dx, dc = offset
        return y_at[dy] + u_at[dx, dc]

    barrier = pltpu.get_barrier_semaphore()
    for offset in near:
        pl.semaphore_signal(barrier, inc=1, device_id=(index_of(offset), z), device_id_type=MESH)
    for k in range(1, nz):
        pl.semaphore_signal(barrier, inc=1, device_id=(ctx, z_peers[k]), device_id_type=MESH)

    for load in loads[3:]:
        load.start()

    def send(src, dst, ssem, rsem, device):
        pltpu.make_async_remote_copy(
            src_ref=src, dst_ref=dst, send_sem=ssem, recv_sem=rsem,
            device_id=device, device_id_type=MESH,
        ).start()

    def rows(ref, index, count):
        return ref.at[pl.ds(pl.multiple_of(index * count, count), count)]

    def wait_for(ref, count, sem):
        pltpu.make_async_copy(ref.at[pl.ds(0, count)], ref.at[pl.ds(0, count)], sem).wait()

    loads[0].wait()
    taps_in = fv[...].astype(F32)
    for to in range(nz):
        for r in range(rr):
            for q in range(q_tiles):
                at = to * width + q * tb
                s0[to * tile + r * q_tiles + q : to * tile + r * q_tiles + q + 1, :] = taps_in[r : r + 1, at : at + tb]

    loads[1].wait()
    loads[2].wait()
    gt[...] = gv[...].astype(F32).T
    xt[...] = xv[...].astype(F32).T
    for j in range(nh):
        sg[j] = gt[pl.ds(j, own, stride=nh), :].astype(BF16)
        sx[j] = xt[pl.ds(j, own, stride=nh), :].astype(BF16)
    pg[n * own :, :] = jnp.zeros((nz * own, 2 * tb), F32)

    pl.semaphore_wait(barrier, len(near) + nz - 1)

    for at, d in enumerate((2, -2)):
        pl.semaphore_signal(gates.at[at], inc=1, device_id=(y_at[d] + u_at[0, 0], z), device_id_type=MESH)
    for k in range(1, nz):
        send(rows(s0, z_peers[k], tile), rows(t1, z, tile), zsend, zrecv, (ctx, z_peers[k]))
    for offset in near:
        peer = index_of(offset)
        part = lax.rem(peer, nh)
        send(sg.at[part], rg.at[ctx], gsend, grecv.at[y], (peer, z))
        if offset[0] != -2:
            send(sx.at[part], rx.at[ctx], xsend, xrecv.at[y], (peer, z))
    rg[pl.ds(ctx, 1)] = sg[pl.ds(mine, 1)]
    rx[pl.ds(ctx, 1)] = sx[pl.ds(mine, 1)]
    t1[pl.ds(pl.multiple_of(z * tile, tile), tile), :] = s0[pl.ds(pl.multiple_of(z * tile, tile), tile), :]

    wait_for(t1, (nz - 1) * tile, zrecv)
    taps = jnp.concatenate([t1[pl.ds(q, nz * rr, stride=q_tiles), :] for q in range(q_tiles)], axis=1)
    all_lanes = rr * lanes
    lane_r = iota((all_lanes, nz * rr), 0) // lanes
    lane_s = iota((all_lanes, nz * rr), 0) % seg // sub
    spread = (iota((all_lanes, nz * rr), 1) == lane_s * rr + lane_r).astype(BF16)
    lane_of = iota((all_lanes, width), 0) % lanes
    own_channel = lane_of // seg * sub + lane_of % sub == iota((all_lanes, width), 1) // nh
    group = (iota((nh, width), 0) == iota((nh, width), 1) % nh).astype(BF16)
    spread_taps = jnp.where(own_channel, dot(spread, taps.astype(BF16), 1, 0), 0.0).astype(BF16)
    for r in range(rr):
        ts[:, r, :] = dot(group, spread_taps[r * lanes : (r + 1) * lanes], 1, 1)
    for at in range(2):
        pl.semaphore_wait(gates.at[at], 1)
    for offset in offsets:
        peer = index_of(offset)
        send(ts.at[lax.rem(peer, nh)], tr.at[ctx], tsend, trecv, (peer, z))
    tr[pl.ds(ctx, 1)] = ts[pl.ds(mine, 1)]

    def to_spectrum(v):
        return dot(jnp.concatenate([v, v], axis=1), fwd[...], 1, 0)

    def thirds(v):
        upper, lower = halves(v)
        return jnp.concatenate([upper, lower, upper], axis=1)

    def from_spectrum(v):
        return dot(thirds(v), inv[...], 1, 0)

    loads[3].wait()
    loads[4].wait()
    loads[5].wait()
    lane = iota((sub, tb), 1)
    parity = jnp.where(lane % 2 == 0, 1.0, -1.0)
    edge = lane == 0
    zero = jnp.zeros((sub, tb), F32)

    def spec_at(ref, block, h):
        at = pl.ds(pl.multiple_of(block * own + h * sub, sub), sub)
        return ref[at, :tb], ref[at, tb:]

    def take(buffer, spectra, sem, k):
        row = y_rows[k]
        wait_for(buffer, nu - 1 if k == 0 else nu, sem.at[row])
        blocks = buffer[pl.ds(row * nu, nu)].reshape(nu * own, tb)
        spectra[pl.ds(pl.multiple_of(row * nu * own, nu * own), nu * own), :] = to_spectrum(blocks)

    def add_row(k, first):
        start = y_rows[k] * nu
        for h in range(hs):
            for d0 in range(0, nz + 1, 3):
                ds = range(d0, min(d0 + 3, nz + 1))
                base = 4 * (nz + 1) * h
                if first:
                    sums = [zero] * (4 * len(ds))
                else:
                    sums = [pacc[base + 4 * d + e] for d in ds for e in range(4)]
                for i in range(0, nu, span):
                    xs = [spec_at(px, start + i + j, h) for j in range(span)]
                    for at in range(ds[0], ds[-1] + span):
                        gr, gi = spec_at(pg, start + i + at, h)
                        for e, d in enumerate(ds):
                            if 0 <= at - d < span:
                                xr, xi = xs[at - d]
                                sums[4 * e] += xr * gr
                                sums[4 * e + 1] += xi * gi
                                sums[4 * e + 2] += xr * gi
                                sums[4 * e + 3] += xi * gr
                for e, d in enumerate(ds):
                    for part in range(4):
                        pacc[base + 4 * d + part] = sums[4 * e + part]

    span = min(4, nu)
    window = (-2, -1, 0, 1)
    taken = set()
    added = set()
    for k in (0, -2, 2, -1, 1):
        take(rg, pg, grecv, k)
        if k in window:
            take(rx, px, xrecv, k)
        taken.add(k)
        for prev in window:
            if prev not in added and prev in taken and prev + 1 in taken:
                add_row(prev, not added)
                added.add(prev)

    def lag(h, d):
        a, b, c, f = [pacc[4 * (nz + 1) * h + 4 * d + e] for e in range(4)]
        return jnp.concatenate([a + jnp.where(edge, 0.0, b), jnp.where(edge, b, c - f)], axis=1)

    signs = jnp.concatenate([parity, parity], axis=1)
    segments = []
    for h in range(hs):
        lags = [lag(h, d) for d in range(nz + 1)]
        segments += [lags[s] + signs * lags[s + 1] for s in range(nz)]
    seg_spec = jnp.concatenate(segments, axis=0)
    by_owner = dot(own_inv[...], thirds(seg_spec), 1, 1)
    for r in range(rr):
        vs[:, r, :] = by_owner[r * n : (r + 1) * n]
    for offset in offsets:
        peer = index_of(offset)
        send(vs.at[peer], vr.at[ctx], vsend, vrecv, (peer, z))
    vr[pl.ds(ctx, 1)] = vs[pl.ds(ctx, 1)]

    wait_for(tr, n - 1, trecv)
    own_taps = jnp.zeros((lanes, tb), F32)
    for r in range(rr):
        place = (iota((n, tb), 1) == iota((n, tb), 0) * rr + r).astype(BF16)
        own_taps = own_taps + dot(tr[:, r, :].T.astype(BF16), place, 1, 0)

    kt[...] = to_spectrum(own_taps.astype(BF16))

    def kernels_of(h):
        found = []
        for d in range(nz + 1):
            real = imag = jnp.zeros((sub, tb), F32)
            at = h * seg + d * sub
            if d < nz:
                real, imag = kt[at : at + sub, :tb], kt[at : at + sub, tb:]
            if d > 0:
                real = real + parity * kt[at - sub : at, :tb]
                imag = imag + parity * kt[at - sub : at, tb:]
            found.append((real, jnp.where(edge, 0.0, imag), jnp.where(edge, imag, real)))
        return found

    for chunk in ((-2, -1), (1, 0)):
        for h in range(hs):
            kernels = kernels_of(h)
            for half_at, k in enumerate(chunk):
                start = y_rows[k] * nu
                for i in range(0, nu, span):
                    real, imag = [zero] * span, [zero] * span
                    for at in range(nz + span):
                        gr, gi = spec_at(pg, start + i + at, h)
                        for j in range(span):
                            if 0 <= at - j <= nz:
                                k1, k2, k3 = kernels[at - j]
                                real[j] += k1 * gr + k2 * gi
                                imag[j] += k3 * gi - k2 * gr
                    for j in range(span):
                        at = (half_at * nu + i + j) * own + h * sub
                        ys[at : at + sub, :tb] = real[j]
                        ys[at : at + sub, tb:] = imag[j]
        outs = from_spectrum(ys[...]).astype(BF16).reshape(len(chunk), nu, own, tb)
        for half_at, k in enumerate(chunk):
            o1[pl.ds(y_rows[k] * nu, nu)] = outs[half_at]
        for offset in offsets:
            if offset[0] in chunk:
                peer = index_of(offset)
                send(o1.at[peer], q2.at[mine], qsend, qrecv, (peer, z))
    q2[pl.ds(mine, 1)] = o1[pl.ds(ctx, 1)]

    wait_for(vr, n - 1, vrecv)
    per_tile = tb // nh
    for r in range(rr):
        vt[r] = (vr[:nh, r, :] + vr[nh:, r, :]).T
        for q in range(q_tiles):
            parts = []
            for e in range(q * per_tile, (q + 1) * per_tile):
                parts.append(vt[r, pl.ds(e // sub * seg + e % sub, nz, stride=sub), :])
            s3[pl.ds(r * q_tiles + q, nz, stride=tile), :] = jnp.concatenate(parts, axis=1)
    for k in range(1, nz):
        send(rows(s3, z_peers[k], tile), rows(o3, z, tile), vzsend, vzrecv, (ctx, z_peers[k]))
    o3[pl.ds(pl.multiple_of(z * tile, tile), tile), :] = s3[pl.ds(pl.multiple_of(z * tile, tile), tile), :]

    wait_for(q2, nh - 1, qrecv)
    for j in range(nh):
        gt[pl.ds(j, own, stride=nh), :] = q2[j].astype(F32)
    out_ref[...] = gt[...].T.astype(BF16)

    wait_for(o3, (nz - 1) * tile, vzrecv)
    for src in range(nz):
        for r in range(rr):
            for q in range(q_tiles):
                at = src * width + q * tb
                row = src * tile + r * q_tiles + q
                tg_ref[r, :, at : at + tb] = o3[row : row + 1, :]

    wait_for(s0, (nz - 1) * tile, zsend)
    wait_for(s3, (nz - 1) * tile, vzsend)
    wait_for(rg, len(near), gsend)
    wait_for(rx, len(near) - nu, xsend)
    wait_for(tr, n - 1, tsend)
    wait_for(vr, n - 1, vsend)
    wait_for(q2, nh - 1, qsend)


def write_out(a_ref, b_ref, a_out, b_out, sem):
    copies = [pltpu.make_async_copy(a_ref, a_out, sem.at[0]), pltpu.make_async_copy(b_ref, b_out, sem.at[1])]
    for copy in copies:
        copy.start()
    for copy in copies:
        copy.wait()


def shards(grad_out, inputs, filter_taps):
    tb, width = grad_out.shape
    n = lax.axis_size("ctx")
    nz = lax.axis_size("ch")
    ny = 8
    nu = n // ny
    nc = 2
    nx = nu // nc
    nh = n // 2
    rr = filter_taps.shape[0]
    own = width // nh
    tile = rr * width // tb
    lanes = own * nz
    vmem = pltpu.VMEM
    dma = pltpu.SemaphoreType.DMA
    results = pl.pallas_call(
        functools.partial(kernel, (n, ny, nx, nc, nz, tb, own, rr)),
        out_shape=(
            pltpu.VMEM((tb, width), BF16),
            pltpu.VMEM((rr, 1, nz * width), F32),
        ),
        in_specs=[pl.BlockSpec(memory_space=pl.ANY)] * 6,
        out_specs=[pl.BlockSpec(memory_space=vmem)] * 2,
        scratch_shapes=[
            vmem((tb, width), BF16),
            vmem((tb, width), BF16),
            vmem((rr, nz * width), BF16),
            vmem((2 * tb, 2 * tb), BF16),
            vmem((6 * tb, tb), BF16),
            vmem((tb, 6 * tb), BF16),
            vmem((width, tb), F32),
            vmem((width, tb), F32),
            vmem((nh, own, tb), BF16),
            vmem((nh, own, tb), BF16),
            vmem((n, own, tb), BF16),
            vmem((n, own, tb), BF16),
            vmem(((n + nz) * own, 2 * tb), F32),
            vmem((n * own, 2 * tb), F32),
            vmem((nz * tile, tb), F32),
            vmem((nz * tile, tb), F32),
            vmem((nh, rr, lanes), F32),
            vmem((n, rr, lanes), F32),
            vmem((own // 8 * 4 * (nz + 1), 8, tb), F32),
            vmem((lanes, 2 * tb), F32),
            vmem((n, rr, lanes), F32),
            vmem((n, rr, lanes), F32),
            vmem((rr, lanes, nh), F32),
            vmem((nz * tile, tb), F32),
            vmem((nz * tile, tb), F32),
            vmem((2 * nu * own, 2 * tb), F32),
            vmem((n, own, tb), BF16),
            vmem((nh, own, tb), BF16),
            pltpu.SemaphoreType.REGULAR((2,)),
            dma((6,)), dma, dma((ny,)), dma, dma((ny,)), dma, dma, dma, dma, dma, dma, dma, dma, dma, dma,
        ],
        compiler_params=pltpu.CompilerParams(collective_id=0, has_side_effects=True),
    )(grad_out, inputs, filter_taps.reshape(rr, nz * width), *dft_tables(tb, rr))
    return pl.pallas_call(
        write_out,
        out_shape=[jax.ShapeDtypeStruct(r.shape, r.dtype) for r in results],
        in_specs=[pl.BlockSpec(memory_space=vmem)] * 2,
        out_specs=[pl.BlockSpec(memory_space=pl.ANY)] * 2,
        scratch_shapes=[dma((2,))],
    )(*[pltpu.with_memory_space_constraint(r, vmem) for r in results])


def solution(mesh):
    placed = (P("ctx", "ch"), P("ctx", "ch"), P("ctx", "ch", None))
    return jax.shard_map(
        shards,
        mesh=mesh,
        in_specs=placed,
        out_specs=(P("ctx", "ch"), P("ctx", "ch", None)),
        check_vma=False,
    )
```

```python
import functools
import jax
import jax.numpy as jnp
import numpy as np
from jax import lax
from jax.experimental import pallas as pl
from jax.experimental.pallas import tpu as pltpu
from jax.sharding import PartitionSpec as P

MESH = pl.DeviceIdType.MESH
F32 = jnp.float32
BF16 = jnp.bfloat16


def iota(shape, axis):
    return lax.broadcasted_iota(jnp.int32, shape, axis)


def dot(a, b, ca, cb):
    return lax.dot_general(a, b, (((ca,), (cb,)), ((), ())), preferred_element_type=F32)


def halves(v):
    upper = v.astype(BF16)
    return upper, (v - upper.astype(F32)).astype(BF16)


def dft_tables(tb, rr):
    place = np.arange(tb)[:, None]
    freq = np.arange(tb)[None, :]
    angle = (place * freq % (2 * tb)) * (np.pi / tb)
    parity = np.where(place % 2 == 0, 1.0, -1.0)
    forward = np.concatenate([np.cos(angle), np.where(freq == 0, parity, -np.sin(angle))], axis=1)
    weight = np.where(np.arange(2 * tb) % tb == 0, 0.5, 1.0) / tb
    backward = (forward * weight).T

    def split(table):
        table = table.astype(np.float32)
        upper = table.astype(BF16)
        return upper, (table - upper.astype(np.float32)).astype(BF16)

    fu, fl = split(forward)
    bu, bl = split(backward)
    inverse = np.concatenate([bu, bu, bl], axis=0)
    by_owner = inverse.T.reshape(tb // rr, rr, 6 * tb).transpose(1, 0, 2).reshape(tb, 6 * tb)
    return np.concatenate([fu, fl], axis=0), inverse, by_owner


def kernel(
    dims, g_hbm, x_hbm, f_hbm, fwd_hbm, inv_hbm, own_hbm, out_ref, tg_ref,
    gv, xv, fv, fwd, inv, own_inv, gt, xt, sg, sx, rg, rx, pg, px,
    s0, t1, ts, tr,
    pacc, kt, vs, vr, vt, s3, o3,
    ys, o1, q2,
    gates, insem, gsend, grecv, xsend, xrecv, zsend, zrecv, tsend, trecv, vsend, vrecv, vzsend, vzrecv, qsend, qrecv,
):
    n, ny, nx, nc, nz, tb, own, rr = dims
    sub = 8
    nu = nx * nc
    nh = n // 2
    hs = own // sub
    width = own * nh
    q_tiles = width // tb
    lanes = own * nz
    seg = sub * nz
    tile = rr * q_tiles

    ctx = lax.axis_index("ctx")
    z = lax.axis_index("ch")
    y = lax.div(ctx, nu)
    x = lax.rem(lax.div(ctx, nc), nx)
    core = lax.rem(ctx, nc)
    mine = lax.rem(ctx, nh)

    loads = [
        pltpu.make_async_copy(f_hbm, fv, insem.at[2]),
        pltpu.make_async_copy(g_hbm, gv, insem.at[0]),
        pltpu.make_async_copy(x_hbm, xv, insem.at[1]),
        pltpu.make_async_copy(fwd_hbm, fwd, insem.at[3]),
        pltpu.make_async_copy(inv_hbm, inv, insem.at[4]),
        pltpu.make_async_copy(own_hbm, own_inv, insem.at[5]),
    ]
    for load in loads[:3]:
        load.start()

    def hops(offset):
        dy, dx, _ = offset
        return abs(dy) + min(dx, nx - dx)

    offsets = [(dy, dx, dc) for dc in range(nc) for dx in range(nx) for dy in range(-3, 5)]
    offsets = sorted([o for o in offsets if any(o)], key=lambda o: -hops(o))
    near = [o for o in offsets if abs(o[0]) <= 2]
    y_rows = {d: lax.rem(y + d + ny, ny) for d in range(-3, 5)}
    y_at = {d: row * nu for d, row in y_rows.items()}
    x_at = [lax.rem(x + d, nx) * nc for d in range(nx)]
    c_at = [lax.rem(core + d, nc) for d in range(nc)]
    u_at = {(dx, dc): x_at[dx] + c_at[dc] for dx in range(nx) for dc in range(nc)}
    z_peers = [lax.rem(z + k, nz) for k in range(nz)]

    def index_of(offset):
        dy, dx, dc = offset
        return y_at[dy] + u_at[dx, dc]

    barrier = pltpu.get_barrier_semaphore()
    for offset in near:
        pl.semaphore_signal(barrier, inc=1, device_id=(index_of(offset), z), device_id_type=MESH)
    for k in range(1, nz):
        pl.semaphore_signal(barrier, inc=1, device_id=(ctx, z_peers[k]), device_id_type=MESH)

    for load in loads[3:]:
        load.start()

    def send(src, dst, ssem, rsem, device):
        pltpu.make_async_remote_copy(
            src_ref=src, dst_ref=dst, send_sem=ssem, recv_sem=rsem,
            device_id=device, device_id_type=MESH,
        ).start()

    def rows(ref, index, count):
        return ref.at[pl.ds(pl.multiple_of(index * count, count), count)]

    def wait_for(ref, count, sem):
        pltpu.make_async_copy(ref.at[pl.ds(0, count)], ref.at[pl.ds(0, count)], sem).wait()

    loads[0].wait()
    taps_in = fv[...].astype(F32)
    for to in range(nz):
        for r in range(rr):
            for q in range(q_tiles):
                at = to * width + q * tb
                s0[to * tile + r * q_tiles + q : to * tile + r * q_tiles + q + 1, :] = taps_in[r : r + 1, at : at + tb]

    loads[1].wait()
    loads[2].wait()
    gt[...] = gv[...].astype(F32).T
    xt[...] = xv[...].astype(F32).T
    for j in range(nh):
        sg[j] = gt[pl.ds(j, own, stride=nh), :].astype(BF16)
        sx[j] = xt[pl.ds(j, own, stride=nh), :].astype(BF16)
    pg[n * own :, :] = jnp.zeros((nz * own, 2 * tb), F32)

    pl.semaphore_wait(barrier, len(near) + nz - 1)

    for at, d in enumerate((2, -2)):
        pl.semaphore_signal(gates.at[at], inc=1, device_id=(y_at[d] + u_at[0, 0], z), device_id_type=MESH)
    for k in range(1, nz):
        send(rows(s0, z_peers[k], tile), rows(t1, z, tile), zsend, zrecv, (ctx, z_peers[k]))
    for offset in near:
        peer = index_of(offset)
        part = lax.rem(peer, nh)
        send(sg.at[part], rg.at[ctx], gsend, grecv.at[2 - offset[0]], (peer, z))
        if offset[0] != -2:
            send(sx.at[part], rx.at[ctx], xsend, xrecv.at[2 - offset[0]], (peer, z))
    rg[pl.ds(ctx, 1)] = sg[pl.ds(mine, 1)]
    rx[pl.ds(ctx, 1)] = sx[pl.ds(mine, 1)]
    t1[pl.ds(pl.multiple_of(z * tile, tile), tile), :] = s0[pl.ds(pl.multiple_of(z * tile, tile), tile), :]

    wait_for(t1, (nz - 1) * tile, zrecv)
    taps = jnp.concatenate([t1[pl.ds(q, nz * rr, stride=q_tiles), :] for q in range(q_tiles)], axis=1)
    all_lanes = rr * lanes
    lane_r = iota((all_lanes, nz * rr), 0) // lanes
    lane_s = iota((all_lanes, nz * rr), 0) % seg // sub
    spread = (iota((all_lanes, nz * rr), 1) == lane_s * rr + lane_r).astype(BF16)
    lane_of = iota((all_lanes, width), 0) % lanes
    own_channel = lane_of // seg * sub + lane_of % sub == iota((all_lanes, width), 1) // nh
    group = (iota((nh, width), 0) == iota((nh, width), 1) % nh).astype(BF16)
    spread_taps = jnp.where(own_channel, dot(spread, taps.astype(BF16), 1, 0), 0.0).astype(BF16)
    per_owner = [dot(group, spread_taps[r * lanes : (r + 1) * lanes], 1, 1) for r in range(rr)]
    ts[...] = jnp.stack(per_owner, axis=1).astype(BF16)
    for at in range(2):
        pl.semaphore_wait(gates.at[at], 1)
    for offset in offsets:
        peer = index_of(offset)
        send(ts.at[lax.rem(peer, nh)], tr.at[ctx], tsend, trecv, (peer, z))
    tr[pl.ds(ctx, 1)] = ts[pl.ds(mine, 1)]

    def to_spectrum(v):
        return dot(jnp.concatenate([v, v], axis=1), fwd[...], 1, 0)

    def thirds(v):
        upper, lower = halves(v)
        return jnp.concatenate([upper, lower, upper], axis=1)

    def from_spectrum(v):
        return dot(thirds(v), inv[...], 1, 0)

    loads[3].wait()
    loads[4].wait()
    loads[5].wait()
    lane = iota((sub, tb), 1)
    parity = jnp.where(lane % 2 == 0, 1.0, -1.0)
    edge = lane == 0
    zero = jnp.zeros((sub, tb), F32)

    def spec_at(ref, block, h):
        at = pl.ds(pl.multiple_of(block * own + h * sub, sub), sub)
        return ref[at, :tb], ref[at, tb:]

    def take(buffer, spectra, sem, k):
        row = y_rows[k]
        wait_for(buffer, nu - 1 if k == 0 else nu, sem.at[k + 2])
        blocks = buffer[pl.ds(row * nu, nu)].reshape(nu * own, tb)
        spectra[pl.ds(pl.multiple_of(row * nu * own, nu * own), nu * own), :] = to_spectrum(blocks)

    def add_rows(k, step, first):
        start = y_rows[k] * nu
        for h in range(hs):
            for d0 in range(0, nz + 1, 3):
                ds = range(d0, min(d0 + 3, nz + 1))
                base = 4 * (nz + 1) * h
                if first:
                    sums = [zero] * (4 * len(ds))
                else:
                    sums = [pacc[base + 4 * d + e] for d in ds for e in range(4)]
                for i in range(0, nu, span):
                    xs = [spec_at(px, start + i + j, h) for j in range(span)]
                    for at in range(ds[0], ds[-1] + span):
                        if (i + at) // nu != step:
                            continue
                        gr, gi = spec_at(pg, start + i + at, h)
                        for e, d in enumerate(ds):
                            if 0 <= at - d < span:
                                xr, xi = xs[at - d]
                                sums[4 * e] += xr * gr
                                sums[4 * e + 1] += xi * gi
                                sums[4 * e + 2] += xr * gi
                                sums[4 * e + 3] += xi * gr
                for e, d in enumerate(ds):
                    for part in range(4):
                        pacc[base + 4 * d + part] = sums[4 * e + part]

    span = min(4, nu)
    window = (-2, -1, 0, 1)
    taken = set()
    added = set()
    for k in (0, -2, 2, -1, 1):
        take(rg, pg, grecv, k)
        if k in window:
            take(rx, px, xrecv, k)
        taken.add(k)
        for at in ((row, step) for row in window for step in range(nz // nu + 1)):
            if at not in added and at[0] in taken and sum(at) in taken:
                add_rows(*at, not added)
                added.add(at)

    def lag(h, d):
        a, b, c, f = [pacc[4 * (nz + 1) * h + 4 * d + e] for e in range(4)]
        return jnp.concatenate([a + jnp.where(edge, 0.0, b), jnp.where(edge, b, c - f)], axis=1)

    signs = jnp.concatenate([parity, parity], axis=1)
    segments = []
    for h in range(hs):
        lags = [lag(h, d) for d in range(nz + 1)]
        segments += [lags[s] + signs * lags[s + 1] for s in range(nz)]
    seg_spec = jnp.concatenate(segments, axis=0)
    by_owner = dot(own_inv[...], thirds(seg_spec), 1, 1)
    for r in range(rr):
        vs[:, r, :] = by_owner[r * n : (r + 1) * n]
    for row in sorted(range(ny), key=lambda r: min(r, ny - r)):
        for dx, dc in u_at:
            peer = row * nu + u_at[dx, dc]
            if dx or dc:
                send(vs.at[peer], vr.at[ctx], vsend, vrecv, (peer, z))
            else:

                @pl.when(y != row)
                def _():
                    send(vs.at[peer], vr.at[ctx], vsend, vrecv, (peer, z))

    vr[pl.ds(ctx, 1)] = vs[pl.ds(ctx, 1)]

    wait_for(tr, n - 1, trecv)
    own_taps = jnp.zeros((lanes, tb), F32)
    arrived = tr[...].astype(F32)
    for r in range(rr):
        place = (iota((n, tb), 1) == iota((n, tb), 0) * rr + r).astype(BF16)
        own_taps = own_taps + dot(arrived[:, r, :].T.astype(BF16), place, 1, 0)

    kt[...] = to_spectrum(own_taps.astype(BF16))

    def kernels_of(h):
        found = []
        for d in range(nz + 1):
            real = imag = jnp.zeros((sub, tb), F32)
            at = h * seg + d * sub
            if d < nz:
                real, imag = kt[at : at + sub, :tb], kt[at : at + sub, tb:]
            if d > 0:
                real = real + parity * kt[at - sub : at, :tb]
                imag = imag + parity * kt[at - sub : at, tb:]
            found.append((real, jnp.where(edge, 0.0, imag), jnp.where(edge, imag, real)))
        return found

    for chunk in ((-2, -1), (1, 0)):
        for h in range(hs):
            kernels = kernels_of(h)
            for half_at, k in enumerate(chunk):
                start = y_rows[k] * nu
                for i in range(0, nu, span):
                    real, imag = [zero] * span, [zero] * span
                    for at in range(nz + span):
                        gr, gi = spec_at(pg, start + i + at, h)
                        for j in range(span):
                            if 0 <= at - j <= nz:
                                k1, k2, k3 = kernels[at - j]
                                real[j] += k1 * gr + k2 * gi
                                imag[j] += k3 * gi - k2 * gr
                    for j in range(span):
                        at = (half_at * nu + i + j) * own + h * sub
                        ys[at : at + sub, :tb] = real[j]
                        ys[at : at + sub, tb:] = imag[j]
        outs = from_spectrum(ys[...]).astype(BF16).reshape(len(chunk), nu, own, tb)
        for half_at, k in enumerate(chunk):
            o1[pl.ds(y_rows[k] * nu, nu)] = outs[half_at]
        for offset in offsets:
            if offset[0] in chunk:
                peer = index_of(offset)
                send(o1.at[peer], q2.at[mine], qsend, qrecv, (peer, z))
    q2[pl.ds(mine, 1)] = o1[pl.ds(ctx, 1)]

    wait_for(vr, n - 1, vrecv)
    per_tile = tb // nh
    for r in range(rr):
        vt[r] = (vr[:nh, r, :] + vr[nh:, r, :]).T
        for q in range(q_tiles):
            parts = []
            for e in range(q * per_tile, (q + 1) * per_tile):
                parts.append(vt[r, pl.ds(e // sub * seg + e % sub, nz, stride=sub), :])
            s3[pl.ds(r * q_tiles + q, nz, stride=tile), :] = jnp.concatenate(parts, axis=1)
    for k in range(1, nz):
        send(rows(s3, z_peers[k], tile), rows(o3, z, tile), vzsend, vzrecv, (ctx, z_peers[k]))
    o3[pl.ds(pl.multiple_of(z * tile, tile), tile), :] = s3[pl.ds(pl.multiple_of(z * tile, tile), tile), :]

    wait_for(q2, nh - 1, qrecv)
    for j in range(nh):
        gt[pl.ds(j, own, stride=nh), :] = q2[j].astype(F32)
    out_ref[...] = gt[...].T.astype(BF16)

    wait_for(o3, (nz - 1) * tile, vzrecv)
    for src in range(nz):
        for r in range(rr):
            for q in range(q_tiles):
                at = src * width + q * tb
                row = src * tile + r * q_tiles + q
                tg_ref[r, :, at : at + tb] = o3[row : row + 1, :]

    wait_for(s0, (nz - 1) * tile, zsend)
    wait_for(s3, (nz - 1) * tile, vzsend)
    wait_for(rg, len(near), gsend)
    wait_for(rx, len(near) - nu, xsend)
    wait_for(tr, n - 1, tsend)
    wait_for(vr, n - 1, vsend)
    wait_for(q2, nh - 1, qsend)


def write_out(a_ref, b_ref, a_out, b_out, sem):
    copies = [pltpu.make_async_copy(a_ref, a_out, sem.at[0]), pltpu.make_async_copy(b_ref, b_out, sem.at[1])]
    for copy in copies:
        copy.start()
    for copy in copies:
        copy.wait()


def shards(grad_out, inputs, filter_taps):
    tb, width = grad_out.shape
    n = lax.axis_size("ctx")
    nz = lax.axis_size("ch")
    ny = 8
    nu = n // ny
    nc = 2
    nx = nu // nc
    nh = n // 2
    rr = filter_taps.shape[0]
    own = width // nh
    tile = rr * width // tb
    lanes = own * nz
    vmem = pltpu.VMEM
    dma = pltpu.SemaphoreType.DMA
    results = pl.pallas_call(
        functools.partial(kernel, (n, ny, nx, nc, nz, tb, own, rr)),
        out_shape=(
            pltpu.VMEM((tb, width), BF16),
            pltpu.VMEM((rr, 1, nz * width), F32),
        ),
        in_specs=[pl.BlockSpec(memory_space=pl.ANY)] * 6,
        out_specs=[pl.BlockSpec(memory_space=vmem)] * 2,
        scratch_shapes=[
            vmem((tb, width), BF16),
            vmem((tb, width), BF16),
            vmem((rr, nz * width), BF16),
            vmem((2 * tb, 2 * tb), BF16),
            vmem((6 * tb, tb), BF16),
            vmem((tb, 6 * tb), BF16),
            vmem((width, tb), F32),
            vmem((width, tb), F32),
            vmem((nh, own, tb), BF16),
            vmem((nh, own, tb), BF16),
            vmem((n, own, tb), BF16),
            vmem((n, own, tb), BF16),
            vmem(((n + nz) * own, 2 * tb), F32),
            vmem((n * own, 2 * tb), F32),
            vmem((nz * tile, tb), F32),
            vmem((nz * tile, tb), F32),
            vmem((nh, rr, lanes), BF16),
            vmem((n, rr, lanes), BF16),
            vmem((own // 8 * 4 * (nz + 1), 8, tb), F32),
            vmem((lanes, 2 * tb), F32),
            vmem((n, rr, lanes), F32),
            vmem((n, rr, lanes), F32),
            vmem((rr, lanes, nh), F32),
            vmem((nz * tile, tb), F32),
            vmem((nz * tile, tb), F32),
            vmem((2 * nu * own, 2 * tb), F32),
            vmem((n, own, tb), BF16),
            vmem((nh, own, tb), BF16),
            pltpu.SemaphoreType.REGULAR((2,)),
            dma((6,)), dma, dma((5,)), dma, dma((4,)), dma, dma, dma, dma, dma, dma, dma, dma, dma, dma,
        ],
        compiler_params=pltpu.CompilerParams(collective_id=0, has_side_effects=True),
    )(grad_out, inputs, filter_taps.reshape(rr, nz * width), *dft_tables(tb, rr))
    return pl.pallas_call(
        write_out,
        out_shape=[jax.ShapeDtypeStruct(r.shape, r.dtype) for r in results],
        in_specs=[pl.BlockSpec(memory_space=vmem)] * 2,
        out_specs=[pl.BlockSpec(memory_space=pl.ANY)] * 2,
        scratch_shapes=[dma((2,))],
    )(*[pltpu.with_memory_space_constraint(r, vmem) for r in results])


def solution(mesh):
    placed = (P("ctx", "ch"), P("ctx", "ch"), P("ctx", "ch", None))
    return jax.shard_map(
        shards,
        mesh=mesh,
        in_specs=placed,
        out_specs=(P("ctx", "ch"), P("ctx", "ch", None)),
        check_vma=False,
    )
```

```python
import functools
import jax
import jax.numpy as jnp
import numpy as np
from jax import lax
from jax.experimental import pallas as pl
from jax.experimental.pallas import tpu as pltpu
from jax.sharding import PartitionSpec as P

MESH = pl.DeviceIdType.MESH
F32 = jnp.float32
BF16 = jnp.bfloat16


def iota(shape, axis):
    return lax.broadcasted_iota(jnp.int32, shape, axis)


def dot(a, b, ca, cb):
    return lax.dot_general(a, b, (((ca,), (cb,)), ((), ())), preferred_element_type=F32)


def halves(v):
    upper = v.astype(BF16)
    return upper, (v - upper.astype(F32)).astype(BF16)


def dft_tables(tb, rr):
    place = np.arange(tb)[:, None]
    freq = np.arange(tb)[None, :]
    angle = (place * freq % (2 * tb)) * (np.pi / tb)
    parity = np.where(place % 2 == 0, 1.0, -1.0)
    forward = np.concatenate([np.cos(angle), np.where(freq == 0, parity, -np.sin(angle))], axis=1)
    weight = np.where(np.arange(2 * tb) % tb == 0, 0.5, 1.0) / tb
    backward = (forward * weight).T

    def split(table):
        table = table.astype(np.float32)
        upper = table.astype(BF16)
        return upper, (table - upper.astype(np.float32)).astype(BF16)

    fu, fl = split(forward)
    bu, bl = split(backward)
    inverse = np.concatenate([bu, bu, bl], axis=0)
    by_owner = inverse.T.reshape(tb // rr, rr, 6 * tb).transpose(1, 0, 2).reshape(tb, 6 * tb)
    return np.concatenate([fu, fl], axis=0), inverse, by_owner


def kernel(
    dims, g_hbm, x_hbm, f_hbm, fwd_hbm, inv_hbm, own_hbm, out_ref, tg_ref,
    gv, xv, fv, fwd, inv, own_inv, gt, xt, sg, sx, rg, rx, pg, px,
    s0, t1, ts, tr,
    pacc, kt, vs, vr, vt, s3, o3,
    ys, o1, q2,
    gates, insem, gsend, grecv, xsend, xrecv, zsend, zrecv, tsend, trecv, vsend, vrecv, vzsend, vzrecv, qsend, qrecv,
):
    n, ny, nx, nc, nz, tb, own, rr = dims
    sub = 8
    nu = nx * nc
    nh = n // 2
    hs = own // sub
    width = own * nh
    q_tiles = width // tb
    lanes = own * nz
    seg = sub * nz
    tile = rr * q_tiles

    ctx = lax.axis_index("ctx")
    z = lax.axis_index("ch")
    y = lax.div(ctx, nu)
    x = lax.rem(lax.div(ctx, nc), nx)
    core = lax.rem(ctx, nc)
    mine = lax.rem(ctx, nh)

    loads = [
        pltpu.make_async_copy(f_hbm, fv, insem.at[2]),
        pltpu.make_async_copy(g_hbm, gv, insem.at[0]),
        pltpu.make_async_copy(x_hbm, xv, insem.at[1]),
        pltpu.make_async_copy(fwd_hbm, fwd, insem.at[3]),
        pltpu.make_async_copy(inv_hbm, inv, insem.at[4]),
        pltpu.make_async_copy(own_hbm, own_inv, insem.at[5]),
    ]
    for load in loads[:3]:
        load.start()

    def hops(offset):
        dy, dx, _ = offset
        return abs(dy) + min(dx, nx - dx)

    offsets = [(dy, dx, dc) for dc in range(nc) for dx in range(nx) for dy in range(-3, 5)]
    offsets = sorted([o for o in offsets if any(o)], key=lambda o: -hops(o))
    near = [o for o in offsets if abs(o[0]) <= 2]
    y_rows = {d: lax.rem(y + d + ny, ny) for d in range(-3, 5)}
    y_at = {d: row * nu for d, row in y_rows.items()}
    x_at = [lax.rem(x + d, nx) * nc for d in range(nx)]
    c_at = [lax.rem(core + d, nc) for d in range(nc)]
    u_at = {(dx, dc): x_at[dx] + c_at[dc] for dx in range(nx) for dc in range(nc)}
    z_peers = [lax.rem(z + k, nz) for k in range(nz)]
    z_far_first = sorted(range(1, nz), key=lambda k: -min(k, nz - k))

    def index_of(offset):
        dy, dx, dc = offset
        return y_at[dy] + u_at[dx, dc]

    barrier = pltpu.get_barrier_semaphore()
    for offset in near:
        pl.semaphore_signal(barrier, inc=1, device_id=(index_of(offset), z), device_id_type=MESH)
    for k in z_far_first:
        pl.semaphore_signal(barrier, inc=1, device_id=(ctx, z_peers[k]), device_id_type=MESH)

    for load in loads[3:]:
        load.start()

    def send(src, dst, ssem, rsem, device):
        pltpu.make_async_remote_copy(
            src_ref=src, dst_ref=dst, send_sem=ssem, recv_sem=rsem,
            device_id=device, device_id_type=MESH,
        ).start()

    def rows(ref, index, count):
        return ref.at[pl.ds(pl.multiple_of(index * count, count), count)]

    def wait_for(ref, count, sem):
        pltpu.make_async_copy(ref.at[pl.ds(0, count)], ref.at[pl.ds(0, count)], sem).wait()

    loads[0].wait()
    taps_in = fv[...].astype(F32)
    for to in range(nz):
        for r in range(rr):
            for q in range(q_tiles):
                at = to * width + q * tb
                s0[to * tile + r * q_tiles + q : to * tile + r * q_tiles + q + 1, :] = taps_in[r : r + 1, at : at + tb]

    loads[1].wait()
    loads[2].wait()
    gt[...] = gv[...].astype(F32).T
    xt[...] = xv[...].astype(F32).T
    for j in range(nh):
        sg[j] = gt[pl.ds(j, own, stride=nh), :].astype(BF16)
        sx[j] = xt[pl.ds(j, own, stride=nh), :].astype(BF16)
    pg[n * own :, :] = jnp.zeros((nz * own, 2 * tb), F32)

    pl.semaphore_wait(barrier, len(near) + nz - 1)

    for at, d in enumerate((2, -2)):
        pl.semaphore_signal(gates.at[at], inc=1, device_id=(y_at[d] + u_at[0, 0], z), device_id_type=MESH)
    for k in z_far_first:
        send(rows(s0, z_peers[k], tile), rows(t1, z, tile), zsend, zrecv, (ctx, z_peers[k]))
    for offset in near:
        peer = index_of(offset)
        part = lax.rem(peer, nh)
        send(sg.at[part], rg.at[ctx], gsend, grecv.at[2 - offset[0]], (peer, z))
        if offset[0] != -2:
            send(sx.at[part], rx.at[ctx], xsend, xrecv.at[2 - offset[0]], (peer, z))
    rg[pl.ds(ctx, 1)] = sg[pl.ds(mine, 1)]
    rx[pl.ds(ctx, 1)] = sx[pl.ds(mine, 1)]
    t1[pl.ds(pl.multiple_of(z * tile, tile), tile), :] = s0[pl.ds(pl.multiple_of(z * tile, tile), tile), :]

    wait_for(t1, (nz - 1) * tile, zrecv)
    taps = jnp.concatenate([t1[pl.ds(q, nz * rr, stride=q_tiles), :] for q in range(q_tiles)], axis=1)
    all_lanes = rr * lanes
    lane_r = iota((all_lanes, nz * rr), 0) // lanes
    lane_s = iota((all_lanes, nz * rr), 0) % seg // sub
    spread = (iota((all_lanes, nz * rr), 1) == lane_s * rr + lane_r).astype(BF16)
    lane_of = iota((all_lanes, width), 0) % lanes
    own_channel = lane_of // seg * sub + lane_of % sub == iota((all_lanes, width), 1) // nh
    group = (iota((nh, width), 0) == iota((nh, width), 1) % nh).astype(BF16)
    spread_taps = jnp.where(own_channel, dot(spread, taps.astype(BF16), 1, 0), 0.0).astype(BF16)
    per_owner = [dot(group, spread_taps[r * lanes : (r + 1) * lanes], 1, 1) for r in range(rr)]
    ts[...] = jnp.stack(per_owner, axis=1).astype(BF16)
    for at in range(2):
        pl.semaphore_wait(gates.at[at], 1)
    for offset in offsets:
        peer = index_of(offset)
        send(ts.at[lax.rem(peer, nh)], tr.at[ctx], tsend, trecv, (peer, z))
    tr[pl.ds(ctx, 1)] = ts[pl.ds(mine, 1)]

    def to_spectrum(v):
        return dot(jnp.concatenate([v, v], axis=1), fwd[...], 1, 0)

    def thirds(v):
        upper, lower = halves(v)
        return jnp.concatenate([upper, lower, upper], axis=1)

    def from_spectrum(v):
        return dot(thirds(v), inv[...], 1, 0)

    loads[3].wait()
    loads[4].wait()
    loads[5].wait()
    lane = iota((sub, tb), 1)
    parity = jnp.where(lane % 2 == 0, 1.0, -1.0)
    edge = lane == 0
    zero = jnp.zeros((sub, tb), F32)

    def spec_at(ref, block, h):
        at = pl.ds(pl.multiple_of(block * own + h * sub, sub), sub)
        return ref[at, :tb], ref[at, tb:]

    def take(buffer, spectra, sem, k):
        row = y_rows[k]
        wait_for(buffer, nu - 1 if k == 0 else nu, sem.at[k + 2])
        blocks = buffer[pl.ds(row * nu, nu)].reshape(nu * own, tb)
        spectra[pl.ds(pl.multiple_of(row * nu * own, nu * own), nu * own), :] = to_spectrum(blocks)

    def add_rows(k, step, first):
        start = y_rows[k] * nu
        for h in range(hs):
            for d0 in range(0, nz + 1, 3):
                ds = range(d0, min(d0 + 3, nz + 1))
                base = 4 * (nz + 1) * h
                if first:
                    sums = [zero] * (4 * len(ds))
                else:
                    sums = [pacc[base + 4 * d + e] for d in ds for e in range(4)]
                for i in range(0, nu, span):
                    xs = [spec_at(px, start + i + j, h) for j in range(span)]
                    for at in range(ds[0], ds[-1] + span):
                        if (i + at) // nu != step:
                            continue
                        gr, gi = spec_at(pg, start + i + at, h)
                        for e, d in enumerate(ds):
                            if 0 <= at - d < span:
                                xr, xi = xs[at - d]
                                sums[4 * e] += xr * gr
                                sums[4 * e + 1] += xi * gi
                                sums[4 * e + 2] += xr * gi
                                sums[4 * e + 3] += xi * gr
                for e, d in enumerate(ds):
                    for part in range(4):
                        pacc[base + 4 * d + part] = sums[4 * e + part]

    span = min(4, nu)
    window = (-2, -1, 0, 1)
    taken = set()
    added = set()
    for k in (0, -2, 2, -1, 1):
        take(rg, pg, grecv, k)
        if k in window:
            take(rx, px, xrecv, k)
        taken.add(k)
        for at in ((row, step) for row in window for step in range(nz // nu + 1)):
            if at not in added and at[0] in taken and sum(at) in taken:
                add_rows(*at, not added)
                added.add(at)

    def lag(h, d):
        a, b, c, f = [pacc[4 * (nz + 1) * h + 4 * d + e] for e in range(4)]
        return jnp.concatenate([a + jnp.where(edge, 0.0, b), jnp.where(edge, b, c - f)], axis=1)

    signs = jnp.concatenate([parity, parity], axis=1)
    segments = []
    for h in range(hs):
        lags = [lag(h, d) for d in range(nz + 1)]
        segments += [lags[s] + signs * lags[s + 1] for s in range(nz)]
    seg_spec = jnp.concatenate(segments, axis=0)
    by_owner = dot(own_inv[...], thirds(seg_spec), 1, 1)
    for r in range(rr):
        vs[:, r, :] = by_owner[r * n : (r + 1) * n]
    for offset in offsets:
        peer = index_of(offset)
        send(vs.at[peer], vr.at[ctx], vsend, vrecv, (peer, z))
    vr[pl.ds(ctx, 1)] = vs[pl.ds(ctx, 1)]

    wait_for(tr, n - 1, trecv)
    own_taps = jnp.zeros((lanes, tb), F32)
    arrived = tr[...].astype(F32)
    for r in range(rr):
        place = (iota((n, tb), 1) == iota((n, tb), 0) * rr + r).astype(BF16)
        own_taps = own_taps + dot(arrived[:, r, :].T.astype(BF16), place, 1, 0)

    kt[...] = to_spectrum(own_taps.astype(BF16))

    def kernels_of(h):
        found = []
        for d in range(nz + 1):
            real = imag = jnp.zeros((sub, tb), F32)
            at = h * seg + d * sub
            if d < nz:
                real, imag = kt[at : at + sub, :tb], kt[at : at + sub, tb:]
            if d > 0:
                real = real + parity * kt[at - sub : at, :tb]
                imag = imag + parity * kt[at - sub : at, tb:]
            found.append((real, jnp.where(edge, 0.0, imag), jnp.where(edge, imag, real)))
        return found

    for chunk in ((-2, -1), (1, 0)):
        for h in range(hs):
            kernels = kernels_of(h)
            for half_at, k in enumerate(chunk):
                start = y_rows[k] * nu
                for i in range(0, nu, span):
                    real, imag = [zero] * span, [zero] * span
                    for at in range(nz + span):
                        gr, gi = spec_at(pg, start + i + at, h)
                        for j in range(span):
                            if 0 <= at - j <= nz:
                                k1, k2, k3 = kernels[at - j]
                                real[j] += k1 * gr + k2 * gi
                                imag[j] += k3 * gi - k2 * gr
                    for j in range(span):
                        at = (half_at * nu + i + j) * own + h * sub
                        ys[at : at + sub, :tb] = real[j]
                        ys[at : at + sub, tb:] = imag[j]
        outs = from_spectrum(ys[...]).astype(BF16).reshape(len(chunk), nu, own, tb)
        for half_at, k in enumerate(chunk):
            o1[pl.ds(y_rows[k] * nu, nu)] = outs[half_at]
        for offset in offsets:
            if offset[0] in chunk:
                peer = index_of(offset)
                send(o1.at[peer], q2.at[mine], qsend, qrecv, (peer, z))
    q2[pl.ds(mine, 1)] = o1[pl.ds(ctx, 1)]

    wait_for(vr, n - 1, vrecv)
    per_tile = tb // nh
    for r in range(rr):
        vt[r] = (vr[:nh, r, :] + vr[nh:, r, :]).T
        for q in range(q_tiles):
            parts = []
            for e in range(q * per_tile, (q + 1) * per_tile):
                parts.append(vt[r, pl.ds(e // sub * seg + e % sub, nz, stride=sub), :])
            s3[pl.ds(r * q_tiles + q, nz, stride=tile), :] = jnp.concatenate(parts, axis=1)
    for k in z_far_first:
        send(rows(s3, z_peers[k], tile), rows(o3, z, tile), vzsend, vzrecv, (ctx, z_peers[k]))
    o3[pl.ds(pl.multiple_of(z * tile, tile), tile), :] = s3[pl.ds(pl.multiple_of(z * tile, tile), tile), :]

    wait_for(q2, nh - 1, qrecv)
    for j in range(nh):
        gt[pl.ds(j, own, stride=nh), :] = q2[j].astype(F32)
    out_ref[...] = gt[...].T.astype(BF16)

    wait_for(o3, (nz - 1) * tile, vzrecv)
    for src in range(nz):
        for r in range(rr):
            for q in range(q_tiles):
                at = src * width + q * tb
                row = src * tile + r * q_tiles + q
                tg_ref[r, :, at : at + tb] = o3[row : row + 1, :]

    wait_for(s0, (nz - 1) * tile, zsend)
    wait_for(s3, (nz - 1) * tile, vzsend)
    wait_for(rg, len(near), gsend)
    wait_for(rx, len(near) - nu, xsend)
    wait_for(tr, n - 1, tsend)
    wait_for(vr, n - 1, vsend)
    wait_for(q2, nh - 1, qsend)


def write_out(a_ref, b_ref, a_out, b_out, sem):
    copies = [pltpu.make_async_copy(a_ref, a_out, sem.at[0]), pltpu.make_async_copy(b_ref, b_out, sem.at[1])]
    for copy in copies:
        copy.start()
    for copy in copies:
        copy.wait()


def shards(grad_out, inputs, filter_taps):
    tb, width = grad_out.shape
    n = lax.axis_size("ctx")
    nz = lax.axis_size("ch")
    ny = 8
    nu = n // ny
    nc = 2
    nx = nu // nc
    nh = n // 2
    rr = filter_taps.shape[0]
    own = width // nh
    tile = rr * width // tb
    lanes = own * nz
    vmem = pltpu.VMEM
    dma = pltpu.SemaphoreType.DMA
    results = pl.pallas_call(
        functools.partial(kernel, (n, ny, nx, nc, nz, tb, own, rr)),
        out_shape=(
            pltpu.VMEM((tb, width), BF16),
            pltpu.VMEM((rr, 1, nz * width), F32),
        ),
        in_specs=[pl.BlockSpec(memory_space=pl.ANY)] * 6,
        out_specs=[pl.BlockSpec(memory_space=vmem)] * 2,
        scratch_shapes=[
            vmem((tb, width), BF16),
            vmem((tb, width), BF16),
            vmem((rr, nz * width), BF16),
            vmem((2 * tb, 2 * tb), BF16),
            vmem((6 * tb, tb), BF16),
            vmem((tb, 6 * tb), BF16),
            vmem((width, tb), F32),
            vmem((width, tb), F32),
            vmem((nh, own, tb), BF16),
            vmem((nh, own, tb), BF16),
            vmem((n, own, tb), BF16),
            vmem((n, own, tb), BF16),
            vmem(((n + nz) * own, 2 * tb), F32),
            vmem((n * own, 2 * tb), F32),
            vmem((nz * tile, tb), F32),
            vmem((nz * tile, tb), F32),
            vmem((nh, rr, lanes), BF16),
            vmem((n, rr, lanes), BF16),
            vmem((own // 8 * 4 * (nz + 1), 8, tb), F32),
            vmem((lanes, 2 * tb), F32),
            vmem((n, rr, lanes), F32),
            vmem((n, rr, lanes), F32),
            vmem((rr, lanes, nh), F32),
            vmem((nz * tile, tb), F32),
            vmem((nz * tile, tb), F32),
            vmem((2 * nu * own, 2 * tb), F32),
            vmem((n, own, tb), BF16),
            vmem((nh, own, tb), BF16),
            pltpu.SemaphoreType.REGULAR((2,)),
            dma((6,)), dma, dma((5,)), dma, dma((4,)), dma, dma, dma, dma, dma, dma, dma, dma, dma, dma,
        ],
        compiler_params=pltpu.CompilerParams(collective_id=0, has_side_effects=True),
    )(grad_out, inputs, filter_taps.reshape(rr, nz * width), *dft_tables(tb, rr))
    return pl.pallas_call(
        write_out,
        out_shape=[jax.ShapeDtypeStruct(r.shape, r.dtype) for r in results],
        in_specs=[pl.BlockSpec(memory_space=vmem)] * 2,
        out_specs=[pl.BlockSpec(memory_space=pl.ANY)] * 2,
        scratch_shapes=[dma((2,))],
    )(*[pltpu.with_memory_space_constraint(r, vmem) for r in results])


def solution(mesh):
    placed = (P("ctx", "ch"), P("ctx", "ch"), P("ctx", "ch", None))
    return jax.shard_map(
        shards,
        mesh=mesh,
        in_specs=placed,
        out_specs=(P("ctx", "ch"), P("ctx", "ch", None)),
        check_vma=False,
    )
```
